128 devices in a mesh: dp: 8 (over y, core), seq: 16 (over x, z).
Axes of the slice: x: 4, y: 4, z: 4, core: 2. Of those that a mesh axis runs over, the one named last changes fastest.
Arguments:
- ssm_input: bfloat16 [8, 4096, 2048], P('dp', 'seq'), may hold values from -6 to 6
- write_basis: bfloat16 [8, 4096, 128], P('dp', 'seq'), may hold values from -2 to 2
- read_basis: bfloat16 [8, 4096, 128], P('dp', 'seq'), may hold values from -2 to 2
- step_size: float32 [8, 4096, 64], P('dp', 'seq')
- log_decay: float32 [8, 4096, 64], P('dp', 'seq')
- head_weight: bfloat16 [2048, 256], replicated, may hold values from -0.125 to 0.125
- block_list: int32 [8, 1024, 16], P('dp', 'seq'), may hold values from 0 to 4095, as said below
- block_count: int32 [8, 1024], P('dp', 'seq'), may hold values from 1 to 16, as said below
- depth_order: int32 [8, 1024, 16], P('dp', 'seq'), may hold values from 0 to 15, each once within a row
- camera_index: int32 [8, 1024], P('dp', 'seq'), may hold values from 0 to 7
- view_gain: float32 [8, 8, 3], P('dp'), may hold values from 0.1 to 1.9
- target_color: float32 [8, 1024, 192], P('dp', 'seq'), may hold values from 0 to 1
Outputs:
- input_grad: bfloat16 [8, 4096, 2048], P('dp', 'seq')
- weight_grad: float32 [2048, 256], replicated
The draws below stay inside these ranges and needn't reach their ends.
Inputs may be any that keep to these rules, and one draw needn't show every extreme that they name: Each scene has a tile whose list holds 16 live slots; slots at block_count or beyond are unused. `depth_order`: each row is a permutation of 0 to 15. `block_list`: entries name tokens of the same scene. Of the 1024 slots of one aligned block of 64 tiles, used or not, at most 128 name tokens of any one aligned block of 256 tokens, and exactly 128 name tokens of some such block.
All inputs are finite; a program needn't handle non-finite values.
Results may differ from the reference program's by a relative error of at most 0.0085.
Values may be sent and summed in bfloat16 or wider, within the bound.
No kernel may reach another device: no remote copies, remote signals or barrier semaphores. Data moves between devices by JAX's collectives and lax.ppermute only.
A program may use at most 128 MiB of HBM per device.

```python
import math
import jax
import jax.numpy as jnp
from jax import lax

SSM_HEAD_COUNT = 64
STATE = 128
GAUSS = 64
BLOCK = 128
LIST = 16
VIEWS = 8
TOK = 256
TILE_DEV = 64
INNER = 2048
FEAT = 256
SCENE_TOKENS = 4096
TILES = 1024
SCENE_COUNT = 8


def head_windows(key):
    pick = jax.random.uniform(jax.random.fold_in(key, 11), (SSM_HEAD_COUNT,))
    slow_share = 0.5
    span_slow = SCENE_TOKENS * jax.random.uniform(jax.random.fold_in(key, 12), (SSM_HEAD_COUNT,), minval=1.0, maxval=2.0)
    span_fast = jax.random.uniform(jax.random.fold_in(key, 13), (SSM_HEAD_COUNT,), minval=30.0, maxval=50.0)
    return jnp.where(pick < slow_share, span_slow, span_fast)


def draw_step_size(key, part):
    token_span = head_windows(key)
    coarse_estimate = jnp.exp(jax.random.uniform(jax.random.fold_in(key, 21), (SCENE_COUNT, SCENE_TOKENS, SSM_HEAD_COUNT), minval=-0.7, maxval=0.7))
    return (coarse_estimate / jnp.sqrt(token_span)[None, None, :]).astype(jnp.float32)


def draw_log_decay(key, part):
    token_span = head_windows(key)
    coarse_estimate = jnp.exp(jax.random.uniform(jax.random.fold_in(key, 31), (SCENE_COUNT, SCENE_TOKENS, SSM_HEAD_COUNT), minval=-0.7, maxval=0.7))
    group_selection = jax.random.uniform(jax.random.fold_in(key, 32), (SCENE_COUNT, SCENE_TOKENS, SSM_HEAD_COUNT))
    group_length = jnp.log(jax.random.uniform(jax.random.fold_in(key, 33), (SCENE_COUNT, SCENE_TOKENS, SSM_HEAD_COUNT), minval=0.5, maxval=0.8))
    token_groups = jnp.where(group_selection < 2.0 / SCENE_TOKENS, group_length, 0.0)
    return (-coarse_estimate / token_span[None, None, :] + token_groups).astype(jnp.float32)


def draw_block_count(key, part):
    counts = jax.random.randint(jax.random.fold_in(key, 41), (SCENE_COUNT, TILES), 1, LIST + 1)
    spot = jax.random.randint(jax.random.fold_in(key, 42), (SCENE_COUNT, 1), 0, TILES)
    return jnp.where(jnp.arange(TILES)[None, :] == spot, LIST, counts).astype(jnp.int32)


def draw_block_list(key, part):
    owners = SCENE_TOKENS // TOK
    slot_total = TILE_DEV * LIST
    limit = 2 * slot_total // owners
    leader = jax.random.randint(jax.random.fold_in(key, 51), (SCENE_COUNT, owners, 1), 0, owners)
    positions = jnp.arange(slot_total, dtype=jnp.int32)
    others = 1 + jnp.maximum(positions - limit, 0) % (owners - 1)
    offset = jnp.where(positions < limit, 0, others)
    owner = (leader + offset[None, None, :]) % owners
    scores = jax.random.randint(jax.random.fold_in(key, 52), (SCENE_COUNT, owners, slot_total), 0, 1048576) * slot_total + positions[None, None, :]
    order = jnp.argsort(scores, axis=2)
    owner = jnp.take_along_axis(owner, order, axis=2)
    local = jax.random.randint(jax.random.fold_in(key, 53), (SCENE_COUNT, owners, slot_total), 0, TOK)
    return (owner * TOK + local).reshape(SCENE_COUNT, TILES, LIST).astype(jnp.int32)


def place_ends(result, stream_key, smallest, high):
    longest = result.shape.index(max(result.shape))
    spots = []
    for shift in (0, 1):
        where = [jax.random.randint(jax.random.fold_in(stream_key, axis), (), 0, length) for axis, length in enumerate(result.shape)]
        where[longest] = (where[longest] + shift) % result.shape[longest]
        spots.append(tuple(where))
    return result.at[spots[0]].set(smallest).at[spots[1]].set(high)


def levels(own_key, shape, shards, least, top_value):
    loudness = 1.0
    for axis_at, shards_of in shards:
        draws = jax.random.uniform(jax.random.fold_in(jax.random.fold_in(own_key, 6), axis_at), (shards_of,), jnp.float32, least / len(shards), top_value / len(shards))
        loudness = loudness * jnp.repeat(jnp.exp(draws), shape[axis_at] // shards_of).reshape((-1,) + (1,) * (len(shape) - 1 - axis_at))
    return loudness


def bell_draw(own_key, extent, scale, reach, cuts=(), kind=jnp.bfloat16):
    entries = jax.random.normal(own_key, extent, jnp.float32) * scale
    if len(cuts) > 0:
        entries = levels(own_key, extent, cuts, -0.22, 0.18) * entries
    return jnp.clip(entries, min=-reach, max=reach).astype(kind)


def setup_inputs(seed: int = 0) -> dict:
    splits = jax.random.split(jax.random.key(seed), 13)
    return {
        "ssm_input": bell_draw(splits[0], (SCENE_COUNT, SCENE_TOKENS, INNER), 1.0, 6.0, ((0, 8), (1, 16))),
        "write_basis": bell_draw(splits[1], (SCENE_COUNT, SCENE_TOKENS, STATE), 0.3, 2.0, ((0, 8), (1, 16))),
        "read_basis": bell_draw(splits[2], (SCENE_COUNT, SCENE_TOKENS, STATE), 0.3, 2.0, ((0, 8), (1, 16))),
        "step_size": draw_step_size(jax.random.fold_in(splits[12], 71), 0),
        "log_decay": draw_log_decay(jax.random.fold_in(splits[12], 71), 0),
        "head_weight": bell_draw(splits[5], (INNER, FEAT), INNER ** -0.5, 0.125),
        "block_list": draw_block_list(jax.random.fold_in(splits[12], 71), 0),
        "block_count": draw_block_count(jax.random.fold_in(splits[12], 71), 0),
        "depth_order": jax.vmap(lambda own: jax.random.permutation(own, LIST))(jax.random.split(splits[8], SCENE_COUNT * TILES)).reshape((SCENE_COUNT, TILES, LIST)).astype(jnp.int32),
        "camera_index": place_ends(jax.random.randint(splits[9], (SCENE_COUNT, TILES), 0, VIEWS), jax.random.fold_in(splits[9], 1), 0, VIEWS - 1).astype(jnp.int32),
        "view_gain": jnp.clip(1.0 + 0.18 * jax.random.normal(splits[10], (SCENE_COUNT, VIEWS, 3), jnp.float32), 0.1, 1.9),
        "target_color": jnp.clip(1.0 * jax.random.uniform(splits[11], (SCENE_COUNT, TILES, 3 * GAUSS), jnp.float32) ** levels(splits[11], (SCENE_COUNT, TILES, 3 * GAUSS), ((0, 8), (1, 16)), -0.2, 0.2), 0.0, 1.0),
    }


HIGHEST = lax.Precision.HIGHEST

def block_fore(carried, pieces):
    scaled_in, write_rows, read_rows, decay_log, write_low, read_low = pieces
    running = jnp.cumsum(decay_log, axis=0)
    positions = jnp.arange(decay_log.shape[0])
    lower_mask = (positions[:, None] >= positions[None, :])[:, :, None]
    spread = jnp.exp(jnp.where(lower_mask, running[:, None, :] - running[None, :, :], -1e+30))
    affinity = jnp.dot(read_low, write_low.T, preferred_element_type=jnp.float32)
    weighted = spread * affinity[:, :, None]
    output = jnp.einsum('ijh,jhp->ihp', weighted, scaled_in, precision=HIGHEST)
    output = output + jnp.exp(running)[:, :, None] * jnp.einsum('in,hnp->ihp', read_rows, carried, precision=HIGHEST)
    tail_decay = jnp.exp(running[-1][None, :] - running)
    next_state = jnp.exp(running[-1])[:, None, None] * carried + jnp.einsum('jn,jhp->hnp', write_rows, scaled_in * tail_decay[:, :, None], precision=HIGHEST)
    return (next_state, output)

def block_back(carried, pieces):
    out_grad, write_rows, read_rows, decay_log, step_rows, write_low, read_low = pieces
    running = jnp.cumsum(decay_log, axis=0)
    positions = jnp.arange(decay_log.shape[0])
    lower_mask = (positions[:, None] >= positions[None, :])[:, :, None]
    spread = jnp.exp(jnp.where(lower_mask, running[:, None, :] - running[None, :, :], -1e+30))
    affinity = jnp.dot(read_low, write_low.T, preferred_element_type=jnp.float32)
    weighted = spread * affinity[:, :, None]
    within = jnp.einsum('uih,uhp->ihp', weighted, out_grad, precision=HIGHEST)
    tail_decay = jnp.exp(running[-1][None, :] - running)
    state_term = tail_decay[:, :, None] * jnp.einsum('in,hnp->ihp', write_rows, carried, precision=HIGHEST)
    input_part = step_rows[:, :, None] * (within + state_term)
    passed = jnp.einsum('un,uhp->hnp', read_rows, out_grad * jnp.exp(running)[:, :, None], precision=HIGHEST)
    passed = passed + jnp.exp(running[-1])[:, None, None] * carried
    return (passed, input_part)

def lookup_gain(camera, gains):
    onehot = (camera[:, None] == jnp.arange(gains.shape[0], dtype=jnp.int32)[None, :]).astype(jnp.float32)
    return lax.optimization_barrier(jnp.sum(onehot[:, :, None] * gains[None, :, :], axis=1))

def composite(slots, depth_rows, block_total, tile_gain, target):
    tile_rows, slot_count, features = slots.shape
    gauss_count = features // 4
    colors = jax.nn.sigmoid(slots[:, :, :3 * gauss_count]).reshape(tile_rows, slot_count, 3, gauss_count)
    opacity = 0.95 * jax.nn.sigmoid(slots[:, :, 3 * gauss_count:])
    live_mask = (depth_rows < block_total[:, None]).astype(jnp.float32)
    color_seq = jnp.take_along_axis(colors, depth_rows[:, :, None, None], axis=1)
    alpha_seq = jnp.take_along_axis(opacity, depth_rows[:, :, None], axis=1) * live_mask[:, :, None]

    def layer_step(running_pair, entry_pair):
        radiance, transmit = running_pair
        color_k, alpha_k = entry_pair
        radiance = radiance + (transmit * alpha_k)[:, None, :] * color_k
        return ((radiance, transmit * (1.0 - alpha_k)), None)
    initial = (jnp.zeros((tile_rows, 3, gauss_count), jnp.float32), jnp.ones((tile_rows, gauss_count), jnp.float32))
    (radiance, _), _ = lax.scan(layer_step, initial, (jnp.moveaxis(color_seq, 1, 0), jnp.moveaxis(alpha_seq, 1, 0)))
    predicted = (radiance * tile_gain[:, :, None]).reshape(tile_rows, 3 * gauss_count)
    residual = predicted - target
    return jnp.sum(jnp.sqrt(residual * residual + 0.01))

def split_blocks(values):
    return values.reshape((values.shape[0] // BLOCK, BLOCK) + values.shape[1:])

def reference(ssm_input, write_basis, read_basis, step_size, log_decay, head_weight, block_list, block_count, depth_order, camera_index, view_gain, target_color):
    heads = step_size.shape[2]
    width = ssm_input.shape[2]
    head_size = width // heads
    length = ssm_input.shape[1]
    state_size = write_basis.shape[2]
    weight_total = jnp.zeros(head_weight.shape, jnp.float32)
    grads = []
    for scene_index in range(SCENE_COUNT):
        write_low = write_basis[scene_index]
        read_low = read_basis[scene_index]
        write_rows = write_low.astype(jnp.float32)
        read_rows = read_low.astype(jnp.float32)
        step_rows = step_size[scene_index]
        decay_log = log_decay[scene_index]
        scaled_in = ssm_input[scene_index].astype(jnp.float32).reshape(length, heads, head_size) * step_rows[:, :, None]
        empty = jnp.zeros((heads, state_size, head_size), jnp.float32)
        _, outputs = lax.scan(block_fore, empty, (split_blocks(scaled_in), split_blocks(write_rows), split_blocks(read_rows), split_blocks(decay_log), split_blocks(write_low), split_blocks(read_low)))
        scan_output = outputs.reshape(length, width).astype(jnp.bfloat16)
        features = jnp.dot(scan_output, head_weight, preferred_element_type=jnp.float32).astype(jnp.bfloat16)
        tile_gain = lookup_gain(camera_index[scene_index], view_gain[scene_index])
        tile_list = block_list[scene_index]
        tile_order = depth_order[scene_index]
        tile_count = block_count[scene_index]
        tile_target = target_color[scene_index]

        def scene_loss(feature_rows):
            return composite(feature_rows[tile_list], tile_order, tile_count, tile_gain, tile_target)
        _, pull = jax.vjp(scene_loss, features.astype(jnp.float32))
        feat_grad = pull(jnp.ones((), jnp.float32))[0]
        feat_low = feat_grad.astype(jnp.bfloat16)
        weight_total = weight_total + lax.dot_general(scan_output, feat_low, (((0,), (0,)), ((), ())), preferred_element_type=jnp.float32)
        out_grad = lax.dot_general(feat_low, head_weight, (((1,), (1,)), ((), ())), preferred_element_type=jnp.float32).astype(jnp.bfloat16)
        out_rows = out_grad.astype(jnp.float32).reshape(length, heads, head_size)
        _, parts = lax.scan(block_back, empty, (split_blocks(out_rows), split_blocks(write_rows), split_blocks(read_rows), split_blocks(decay_log), split_blocks(step_rows), split_blocks(write_low), split_blocks(read_low)), reverse=True)
        grads.append(parts.reshape(length, width).astype(jnp.bfloat16))
    return (jnp.stack(grads), weight_total / math.sqrt(SCENE_COUNT * length))
```

```python
import jax
import jax.numpy as jnp
import numpy as np
from jax import lax
from jax.experimental import pallas as pl
from jax.experimental.pallas import tpu as pltpu
from jax.sharding import Mesh
from jax.sharding import PartitionSpec as P

SEQ = ("seq_0", "seq_1")
F32 = jnp.float32
BF16 = jnp.bfloat16
NEG = -1e30
LOG2E = 1.4426950408889634

OWN = 16
TOK = 256
BLK = 128
NST = 128
HEADS = 64
WID = 2048
FEAT = 256
CH = 256
NCH = WID // CH
TILES = 64
SLOTS = 16
ROWS = TILES * SLOTS
TAIL = 16


def dot(a, b):
    return lax.dot_general(a, b, (((1,), (0,)), ((), ())), preferred_element_type=F32)


def dot_t(a, b):
    return lax.dot_general(a, b, (((1,), (1,)), ((), ())), preferred_element_type=F32)


def iota(shape, dim):
    return lax.broadcasted_iota(jnp.int32, shape, dim)


def turned(a):
    return a.astype(F32).T.astype(BF16)


def split_pair(f):
    high = f.astype(BF16).astype(F32)
    return jnp.where(iota(f.shape, 1) < HEADS, high, f - high).astype(BF16)


def spreader():
    return (iota((2 * HEADS, CH), 0) & (HEADS - 1)) - (iota((2 * HEADS, CH), 1) >> 5)


def spread_of(base, c):
    return (base == 8 * c).astype(F32).astype(BF16)


def cols(c):
    return slice(c * CH, (c + 1) * CH)


def call(body, outs, scratch=(), in_specs=None, out_specs=None, limit=32, flops=0, grid=None, alias=None):
    kwargs = {}
    if in_specs is not None:
        kwargs["in_specs"] = in_specs
    if out_specs is not None:
        kwargs["out_specs"] = out_specs
    if grid is not None:
        kwargs["grid"] = grid
    return pl.pallas_call(
        body,
        out_shape=[jax.ShapeDtypeStruct(s, d) for s, d in outs],
        scratch_shapes=list(scratch),
        compiler_params=pltpu.CompilerParams(vmem_limit_bytes=limit << 20),
        cost_estimate=pl.CostEstimate(flops=flops, transcendentals=0, bytes_accessed=4 << 20),
        input_output_aliases=alias or {},
        **kwargs,
    )


def local_end_body(x, wr, step, logd, pay, run_out, step_out):
    ld = jnp.concatenate([logd[...], logd[...]], axis=1)
    st = jnp.concatenate([step[...], step[...]], axis=1)
    row = iota((TOK, 2 * HEADS), 0)
    run = ld
    s = 1
    while s < TOK:
        run = run + jnp.where(row >= s, pltpu.roll(run, s, 0), 0.0)
        s *= 2
    run_out[...] = run
    step_out[...] = st
    total = run[TOK - 1 : TOK, :]
    pair = split_pair(st * jnp.exp(total - run))
    t1 = total.astype(BF16).astype(F32)
    t2 = (total - t1).astype(BF16).astype(F32)
    t3 = total - t1 - t2
    trow = iota((TAIL, 2 * HEADS), 0)
    tails = jnp.where(trow == 0, t1, jnp.where(trow == 1, t2, jnp.where(trow == 2, t3, 0.0)))
    tails = jnp.where(iota((TAIL, 2 * HEADS), 1) < HEADS, tails, 0.0).astype(BF16)
    wt = turned(wr[...])
    base = spreader()
    for c in range(NCH):
        e = spread_of(base, c)
        xs = (x[:, cols(c)].astype(F32) * dot(pair, e)).astype(BF16)
        end = dot(wt, xs).astype(BF16)
        extra = dot(tails, e).astype(BF16)
        for k in range(2):
            lanes = slice(k * 128, (k + 1) * 128)
            pay[2 * c + k, 0:NST, :] = end[:, lanes]
            pay[2 * c + k, NST : NST + TAIL, :] = extra[:, lanes]


def decayed(tail):
    return jnp.exp(
        tail[0:1, :].astype(F32) + tail[1:2, :].astype(F32) + tail[2:3, :].astype(F32)
    )


def prefix_body(got, asks, pay):
    state = jnp.zeros((NST, 128), F32)
    for d in range(OWN):
        pay[d, 0:NST, :] = state.astype(BF16)
        pay[d, NST : NST + TAIL, :] = asks[d]
        if d < OWN - 1:
            decay = decayed(got[d, NST : NST + TAIL, :])
            state = decay * state + got[d, 0:NST, :].astype(F32)


def head_weights(run_rows, run_lanes, h, lanes, mask, aff, forward):
    a = run_rows[:, h : h + 1]
    b = run_lanes[h : h + 1, lanes]
    gap = a - b if forward else b - a
    return (jnp.exp2(jnp.where(mask, gap, NEG)) * aff).astype(BF16)


def lane_masks():
    which = iota((BLK, 128), 1) >> 5
    return [(which == q).astype(F32).astype(BF16) for q in range(4)]


def group_out(run_rows, run_lanes, first, lanes, mask, aff, values, masks, forward):
    ws = [
        head_weights(run_rows, run_lanes, first + q, lanes, mask, aff, forward) for q in range(4)
    ]
    return dot(
        jnp.concatenate(ws, axis=1), jnp.concatenate([values * m for m in masks], axis=0)
    )


def fore_local_body(x, wr, rd, run, step, out, mid):
    run2 = run[...] * LOG2E
    run_lanes = run2.T
    masks = lane_masks()
    mask = iota((BLK, BLK), 0) >= iota((BLK, BLK), 1)
    base = spreader()
    step_pair = split_pair(step[...])
    edge = run2[BLK - 1 : BLK, :]
    for b in range(2):
        rows = slice(b * BLK, (b + 1) * BLK)
        run_rows = run2[rows, :]
        aff = dot_t(rd[rows, :], wr[rows, :])
        if b == 0:
            side = split_pair(step[rows, :] * jnp.exp2(edge - run_rows))
            wt = turned(wr[rows, :])
        else:
            side = split_pair(jnp.exp2(run_rows - edge))
        for c in range(NCH):
            e = spread_of(base, c)
            xs = x[rows, cols(c)].astype(F32)
            values = (xs * dot(step_pair[rows, :], e)).astype(BF16)
            sides = dot(side, e)
            if b == 0:
                mid[:, cols(c)] = dot(wt, (xs * sides).astype(BF16)).astype(BF16)
            else:
                carried = sides * dot(rd[rows, :], mid[:, cols(c)])
            for k in range(2):
                lanes = slice(k * 128, (k + 1) * 128)
                o = group_out(
                    run_rows, run_lanes, 8 * c + 4 * k, rows, mask, aff, values[:, lanes], masks, True
                )
                if b == 1:
                    o = o + carried[:, lanes]
                out[rows, c * CH + k * 128 : c * CH + (k + 1) * 128] = o


def back_local_body(og, wr, rd, run, out, mid):
    run2 = run[...] * LOG2E
    run_lanes = run2.T
    masks = lane_masks()
    mask = iota((BLK, BLK), 0) <= iota((BLK, BLK), 1)
    base = spreader()
    edge = run2[BLK - 1 : BLK, :]
    for b in (1, 0):
        rows = slice(b * BLK, (b + 1) * BLK)
        run_rows = run2[rows, :]
        aff = dot_t(wr[rows, :], rd[rows, :])
        if b == 1:
            side = split_pair(jnp.exp2(run_rows - edge))
            rt = turned(rd[rows, :])
        else:
            side = split_pair(jnp.exp2(edge - run_rows))
        for c in range(NCH):
            e = spread_of(base, c)
            values = og[rows, cols(c)]
            sides = dot(side, e)
            if b == 1:
                mid[:, cols(c)] = dot(rt, (values.astype(F32) * sides).astype(BF16)).astype(BF16)
            else:
                carried = sides * dot(wr[rows, :], mid[:, cols(c)])
            for k in range(2):
                lanes = slice(k * 128, (k + 1) * 128)
                o = group_out(
                    run_rows, run_lanes, 8 * c + 4 * k, rows, mask, aff, values[:, lanes], masks, False
                )
                if b == 0:
                    o = o + carried[:, lanes]
                out[rows, c * CH + k * 128 : c * CH + (k + 1) * 128] = o


def places_body(ids, depth, asks, place_col, place_row):
    idv = ids[...].astype(F32)
    dep = depth[...]
    seq = jnp.zeros((TILES, SLOTS), F32)
    for s in range(SLOTS):
        seq = seq + jnp.where(dep == s, idv[:, s : s + 1], 0.0)
    lane = iota((128, 128), 1)
    lane_f = lane.astype(F32)
    below = (iota((128, 128), 0) > lane).astype(F32).astype(BF16)
    seen = jnp.zeros((1, 128), F32)
    total = jnp.zeros((128, 128), F32)
    for b in range(ROWS // 128):
        two = [jnp.broadcast_to(seq[:, k : k + 1], (TILES, 128)) for k in (2 * b, 2 * b + 1)]
        token = jnp.concatenate(two, axis=0).astype(jnp.int32)
        owner = token >> 8
        local = (token & 255).astype(F32)
        hot = owner == lane
        hot_f = hot.astype(F32)
        rank = dot(below, hot_f.astype(BF16)) + seen
        seen = seen + jnp.sum(hot_f, axis=0, keepdims=True)
        mine = jnp.sum(jnp.where(hot, rank, 0.0), axis=1, keepdims=True)
        mine = jnp.broadcast_to(mine, (128, 128))
        place = mine + (owner * 128).astype(F32)
        place_col[b * 128 : (b + 1) * 128, :] = place
        place_row[:, b * 128 : (b + 1) * 128] = place.T[0:8, :]
        named = jnp.where(hot, local, 0.0)
        total = total + dot(turned(named), (mine == lane_f).astype(F32).astype(BF16))
    first = iota((TAIL, 128), 0) == 0
    for o in range(OWN):
        asks[o] = jnp.where(first, total[o : o + 1, :], 0.0).astype(BF16)


def features_body(local, got, rd, run, weight, scan_out, answer):
    base = spreader()
    lead = split_pair(jnp.exp(run[...]))
    feat = jnp.zeros((TOK, FEAT), F32)
    for c in range(NCH):
        state = jnp.concatenate([got[2 * c, 0:NST, :], got[2 * c + 1, 0:NST, :]], axis=1)
        rows = local[:, cols(c)] + dot(lead, spread_of(base, c)) * dot(rd[...], state)
        rows = rows.astype(BF16)
        scan_out[:, cols(c)] = rows
        feat = feat + dot(rows, weight[cols(c), :])
    feat = feat.astype(BF16)
    asked = jnp.concatenate(
        [got[d, NST : NST + TAIL, :].astype(F32)[0:1, :] for d in range(OWN)]
        + [jnp.zeros((128 - OWN, 128), F32)],
        axis=0,
    ).T
    token = iota((128, TOK), 1).astype(F32)
    for d in range(OWN):
        pick = (asked[:, d : d + 1] == token).astype(F32).astype(BF16)
        answer[d] = dot(pick, feat).astype(BF16)


def composite_body(
    ans, place_col, place_row, depth, count, camera, gain, target, out, slots, keep, trans, grads
):
    lane_f = iota((256, 128), 1).astype(F32)
    for b in range(ROWS // 256):
        rows = slice(b * 256, (b + 1) * 256)
        place = place_col[rows, :]
        hot = jnp.concatenate(
            [(place == lane_f + 128.0 * o).astype(F32).astype(BF16) for o in range(OWN)], axis=1
        )
        slots[rows, :] = dot(hot, ans[...])
    lane = iota((TILES, 128), 1)
    left = lane < GAUSS_LANES
    dep = depth[...]
    cnt = count[...]
    cam = camera[...]
    vg = gain[...]
    wide = iota((8, FEAT), 1)
    gains = jnp.where(wide < 64, vg[:, 0:1], jnp.where(wide < 128, vg[:, 1:2], vg[:, 2:3]))
    tile_gain = jnp.zeros((TILES, FEAT), F32)
    for v in range(8):
        tile_gain = tile_gain + jnp.where(cam == v, gains[v : v + 1, :], 0.0)
    gain_a, gain_b = tile_gain[:, 0:128], tile_gain[:, 128:256]
    target_a = target[:, 0:128]
    target_b = jnp.concatenate([target[:, 128:192], jnp.zeros((TILES, 64), F32)], axis=1)
    t = jnp.ones((TILES, 128), F32)
    ra = jnp.zeros((TILES, 128), F32)
    rb = jnp.zeros((TILES, 128), F32)
    for k in range(SLOTS):
        rows = slice(k * TILES, (k + 1) * TILES)
        sa = jax.nn.sigmoid(slots[rows, 0:128])
        sb = jax.nn.sigmoid(slots[rows, 128:256])
        so = jnp.where(left, pltpu.roll(sb, 64, 1), sb)
        live = jnp.where(dep[:, k : k + 1] < cnt, 0.95, 0.0)
        a = so * live
        w = t * a
        ra = ra + w * sa
        rb = rb + w * sb
        slots[rows, 0:128] = sa
        slots[rows, 128:256] = sb
        keep[rows, :] = so
        trans[rows, :] = t
        t = t * (1.0 - a)
    ea = ra * gain_a - target_a
    eb = rb * gain_b - target_b
    ga = ea * lax.rsqrt(ea * ea + 0.01) * gain_a
    gb = jnp.where(left, eb * lax.rsqrt(eb * eb + 0.01) * gain_b, 0.0)
    dt = jnp.zeros((TILES, 128), F32)
    for k in reversed(range(SLOTS)):
        rows = slice(k * TILES, (k + 1) * TILES)
        sa = slots[rows, 0:128]
        sb = slots[rows, 128:256]
        so = keep[rows, :]
        t = trans[rows, :]
        live = jnp.where(dep[:, k : k + 1] < cnt, 0.95, 0.0)
        a = so * live
        ua = ga * sa
        ub = gb * sb
        q = ua + ub
        q = q + pltpu.roll(q, 64, 1)
        da = t * (q - dt)
        dt = a * q + (1.0 - a) * dt
        w = t * a
        grads[rows, 0:128] = (w * ua * (1.0 - sa)).astype(BF16)
        grads[rows, 128:256] = jnp.where(
            left, w * ub * (1.0 - sb), da * a * (1.0 - so)
        ).astype(BF16)
    sub_f = iota((256, ROWS), 0).astype(F32)
    place = place_row[0:1, :]
    for b in range(OWN * 128 // 256):
        hot = (place == sub_f + 256.0 * b).astype(F32).astype(BF16)
        out[b * 256 : (b + 1) * 256, :] = dot(hot, grads[...]).astype(BF16)


GAUSS_LANES = 64


def token_grad_body(homed, asked, weight, scan_out, rd, run, out_grad, pay):
    token = iota((TOK, 128), 0).astype(F32)
    hot = jnp.concatenate(
        [
            (asked[d].astype(F32)[0:1, :] == token).astype(F32).astype(BF16)
            for d in range(OWN)
        ],
        axis=1,
    )
    feat = dot(hot, homed[...])
    low = feat.astype(BF16)
    low_t = turned(low)
    base = spreader()
    lead = split_pair(jnp.exp(run[...]))
    rt = turned(rd[...])
    for c in range(NCH):
        og = dot_t(low, weight[cols(c), :]).astype(BF16)
        out_grad[:, cols(c)] = og
        scaled = (og.astype(F32) * dot(lead, spread_of(base, c))).astype(BF16)
        end = dot(rt, scaled).astype(BF16)
        part = dot(low_t, scan_out[:, cols(c)]).astype(BF16)
        for k in range(2):
            lanes = slice(k * 128, (k + 1) * 128)
            pay[2 * c + k, 0:NST, :] = end[:, lanes]
            pay[2 * c + k, NST : NST + FEAT, :] = part[:, lanes]


def scene_sum_body(got, out):
    total = jnp.zeros((FEAT, 128), F32)
    for d in range(OWN):
        total = total + got[d, NST : NST + FEAT, :].astype(F32)
    total = total.astype(BF16)
    for i in range(8):
        out[i] = total


def suffix_body(got, tails, pay):
    state = jnp.zeros((NST, 128), F32)
    for d in reversed(range(OWN)):
        pay[d, 0:NST, :] = state.astype(BF16)
        if d > 0:
            state = decayed(tails[d]) * state + got[d, 0:NST, :].astype(F32)


def all_scenes_body(scale, parts, pay_in, pay):
    del pay_in
    total = parts[0].astype(F32)
    for i in range(1, 8):
        total = total + parts[i].astype(F32)
    total = (total * scale).T
    half = total[:, 0:128].astype(BF16)
    other = total[:, 128:256].astype(BF16)
    first = pl.program_id(0) == 0
    block = jnp.where(first, half.astype(F32), other.astype(F32)).astype(BF16)
    for d in range(OWN):
        pay[d] = block


def input_grad_body(within, got, wr, run, step, grad, wgrad):
    base = spreader()
    run_v = run[...]
    tail = split_pair(jnp.exp(run_v[TOK - 1 : TOK, :] - run_v))
    steps = split_pair(step[...])
    for c in range(NCH):
        e = spread_of(base, c)
        state = jnp.concatenate([got[2 * c, 0:NST, :], got[2 * c + 1, 0:NST, :]], axis=1)
        rows = within[:, cols(c)] + dot(tail, e) * dot(wr[...], state)
        grad[:, cols(c)] = (rows * dot(steps, e)).astype(BF16)
    for d in range(OWN):
        wgrad[d * 128 : (d + 1) * 128, 0:128] = got[d, NST : NST + 128, :].astype(F32)
        wgrad[d * 128 : (d + 1) * 128, 128:256] = got[d, NST + 128 : NST + 256, :].astype(F32)


def swap(x, axes):
    return lax.all_to_all(x, axes, split_axis=0, concat_axis=0, tiled=True)


def shards(
    ssm_input,
    write_basis,
    read_basis,
    step_size,
    log_decay,
    head_weight,
    block_list,
    block_count,
    depth_order,
    camera_index,
    view_gain,
    target_color,
):
    x, wr, rd = ssm_input[0], write_basis[0], read_basis[0]
    depth = depth_order[0]
    tail_spec = pl.BlockSpec((OWN, TAIL, 128), lambda *_: (0, NST // TAIL, 0))
    vmem = pl.BlockSpec(memory_space=pltpu.VMEM)

    pay, run, step = call(
        local_end_body,
        [((OWN, NST + TAIL, 128), BF16), ((TOK, 128), F32), ((TOK, 128), F32)],
        flops=1 << 29,
    )(x, wr, step_size[0], log_decay[0])
    ends = swap(pay, SEQ)
    asks, place_col, place_row = call(
        places_body,
        [((OWN, TAIL, 128), BF16), ((ROWS, 128), F32), ((8, ROWS), F32)],
        flops=1 << 31,
    )(block_list[0], depth)
    (local,) = call(
        fore_local_body,
        [((TOK, WID), F32)],
        scratch=[pltpu.VMEM((NST, WID), BF16)],
        flops=1 << 32,
    )(x, wr, rd, run, step)
    (pay,) = call(prefix_body, [((OWN, NST + TAIL, 128), BF16)])(ends, asks)
    states = swap(pay, SEQ)
    scan_out, answer = call(
        features_body, [((TOK, WID), BF16), ((OWN, 128, FEAT), BF16)], flops=1 << 31
    )(local, states, rd, run, head_weight)
    answered = swap(answer, SEQ)
    (outgoing,) = call(
        composite_body,
        [((OWN * 128, FEAT), BF16)],
        scratch=[
            pltpu.VMEM((ROWS, FEAT), F32),
            pltpu.VMEM((ROWS, 128), F32),
            pltpu.VMEM((ROWS, 128), F32),
            pltpu.VMEM((ROWS, FEAT), BF16),
        ],
        flops=1 << 32,
    )(
        answered.reshape(OWN * 128, FEAT),
        place_col,
        place_row,
        depth,
        block_count[0][:, None],
        camera_index[0][:, None],
        view_gain[0],
        target_color[0],
    )
    homed = swap(outgoing.reshape(OWN, 128, FEAT), SEQ)
    out_grad, pay = call(
        token_grad_body,
        [((TOK, WID), BF16), ((OWN, NST + FEAT, 128), BF16)],
        in_specs=[vmem, tail_spec, vmem, vmem, vmem, vmem],
        out_specs=[vmem, vmem],
        grid=(1,),
        flops=1 << 31,
    )(homed.reshape(OWN * 128, FEAT), states, head_weight, scan_out, rd, run)
    back = swap(pay, SEQ)
    (within,) = call(
        back_local_body,
        [((TOK, WID), F32)],
        scratch=[pltpu.VMEM((NST, WID), BF16)],
        flops=1 << 32,
    )(out_grad, wr, rd, run)
    (scene_part,) = call(scene_sum_body, [((8, FEAT, 128), BF16)])(back)
    scene_parts = swap(scene_part, ("dp",))
    (pay,) = call(
        suffix_body,
        [((OWN, NST + FEAT, 128), BF16)],
        in_specs=[pl.BlockSpec((OWN, NST, 128), lambda *_: (0, 0, 0)), tail_spec],
        out_specs=[pl.BlockSpec((OWN, NST, 128), lambda *_: (0, 0, 0))],
        grid=(1,),
    )(back, ends)
    scale = 1.0 / np.sqrt(np.float64(lax.axis_size("dp") * TOK * lax.axis_size(SEQ)))
    (pay,) = call(
        lambda *refs: all_scenes_body(np.float32(scale), *refs),
        [((OWN, NST + FEAT, 128), BF16)],
        in_specs=[vmem, pl.BlockSpec(memory_space=pl.ANY)],
        out_specs=[pl.BlockSpec((OWN, 128, 128), lambda i: (0, 1 + i, 0))],
        grid=(2,),
        alias={1: 0},
    )(scene_parts, pay)
    states_back = swap(pay, SEQ)
    grad, wgrad = call(
        input_grad_body, [((TOK, WID), BF16), ((WID, FEAT), F32)], flops=1 << 30
    )(within, states_back, wr, run, step)
    return grad[None], wgrad


def solution(mesh):
    torus = Mesh(mesh.devices.reshape(mesh.shape["dp"], 4, 4), ("dp", "seq_0", "seq_1"))
    in_specs = (
        P("dp", SEQ, None),
        P("dp", SEQ, None),
        P("dp", SEQ, None),
        P("dp", SEQ, None),
        P("dp", SEQ, None),
        P(),
        P("dp", SEQ, None),
        P("dp", SEQ),
        P("dp", SEQ, None),
        P("dp", SEQ),
        P("dp", None, None),
        P("dp", SEQ, None),
    )
    out_specs = (P("dp", SEQ, None), P())
    return jax.shard_map(
        shards, mesh=torus, in_specs=in_specs, out_specs=out_specs, check_vma=False
    )
```

```python
import jax
import jax.numpy as jnp
import numpy as np
from jax import lax
from jax.experimental import pallas as pl
from jax.experimental.pallas import tpu as pltpu
from jax.sharding import Mesh
from jax.sharding import PartitionSpec as P

SEQ = ("seq_0", "seq_1")
F32 = jnp.float32
BF16 = jnp.bfloat16
NEG = -1e30
LOG2E = 1.4426950408889634

OWN = 16
TOK = 256
BLK = 128
NST = 128
HEADS = 64
WID = 2048
FEAT = 256
CH = 256
NCH = WID // CH
TILES = 64
SLOTS = 16
ROWS = TILES * SLOTS
TAIL = 16


def dot(a, b):
    return lax.dot_general(a, b, (((1,), (0,)), ((), ())), preferred_element_type=F32)


def dot_t(a, b):
    return lax.dot_general(a, b, (((1,), (1,)), ((), ())), preferred_element_type=F32)


def iota(shape, dim):
    return lax.broadcasted_iota(jnp.int32, shape, dim)


def turned(a):
    return a.astype(F32).T.astype(BF16)


def split_pair(f):
    high = f.astype(BF16).astype(F32)
    return jnp.where(iota(f.shape, 1) < HEADS, high, f - high).astype(BF16)


def spreader():
    return (iota((2 * HEADS, CH), 0) & (HEADS - 1)) - (iota((2 * HEADS, CH), 1) >> 5)


def spread_of(base, c):
    return (base == 8 * c).astype(F32).astype(BF16)


def cols(c):
    return slice(c * CH, (c + 1) * CH)


ANY = pl.BlockSpec(memory_space=pl.ANY)
VMEM = pl.BlockSpec(memory_space=pltpu.VMEM)
TAIL_SPEC = pl.BlockSpec((OWN, TAIL, 128), lambda *_: (0, NST // TAIL, 0))


def near(shape, dtype):
    return pltpu.VMEM(shape, dtype)


def held(x):
    return pltpu.with_memory_space_constraint(x, pltpu.VMEM)


def far(x):
    return pltpu.with_memory_space_constraint(x, pltpu.HBM)


def call(body, outs, ins, out_specs, scratch=(), limit=16, flops=0, grid=()):
    return pl.pallas_call(
        body,
        out_shape=[
            (near if len(o) == 3 else jax.ShapeDtypeStruct)(o[0], o[1]) for o in outs
        ],
        grid_spec=pl.GridSpec(
            grid=grid, in_specs=ins, out_specs=out_specs, scratch_shapes=list(scratch)
        ),
        compiler_params=pltpu.CompilerParams(vmem_limit_bytes=limit << 20),
        cost_estimate=pl.CostEstimate(flops=flops, transcendentals=0, bytes_accessed=4 << 20),
    )


def local_end_body(
    x_far, wr_far, step_far, logd_far, pay, run_out, step_out, x, wr, step, logd, sem
):
    moves = [
        pltpu.make_async_copy(a, b, sem.at[k])
        for k, (a, b) in enumerate(
            ((logd_far, logd), (step_far, step), (wr_far, wr), (x_far, x))
        )
    ]
    for m in moves:
        m.start()
    moves[0].wait()
    moves[1].wait()
    ld = jnp.concatenate([logd[...], logd[...]], axis=0).T
    st = jnp.concatenate([step[...], step[...]], axis=0).T
    row = iota((TOK, 2 * HEADS), 0)
    run = ld
    s = 1
    while s < TOK:
        run = run + jnp.where(row >= s, pltpu.roll(run, s, 0), 0.0)
        s *= 2
    run_out[...] = run
    step_out[...] = st
    total = run[TOK - 1 : TOK, :]
    pair = split_pair(st * jnp.exp(total - run))
    t1 = total.astype(BF16).astype(F32)
    t2 = (total - t1).astype(BF16).astype(F32)
    t3 = total - t1 - t2
    trow = iota((TAIL, 2 * HEADS), 0)
    tails = jnp.where(trow == 0, t1, jnp.where(trow == 1, t2, jnp.where(trow == 2, t3, 0.0)))
    tails = jnp.where(iota((TAIL, 2 * HEADS), 1) < HEADS, tails, 0.0).astype(BF16)
    moves[2].wait()
    wt = turned(wr[...])
    base = spreader()
    moves[3].wait()
    for c in range(NCH):
        e = spread_of(base, c)
        xs = (x[:, cols(c)].astype(F32) * dot(pair, e)).astype(BF16)
        end = dot(wt, xs).astype(BF16)
        extra = dot(tails, e).astype(BF16)
        for k in range(2):
            lanes = slice(k * 128, (k + 1) * 128)
            pay[2 * c + k, 0:NST, :] = end[:, lanes]
            pay[2 * c + k, NST : NST + TAIL, :] = extra[:, lanes]


def decayed(tail):
    return jnp.exp(
        tail[0:1, :].astype(F32) + tail[1:2, :].astype(F32) + tail[2:3, :].astype(F32)
    )


def prefix_body(got, asks, pay):
    state = jnp.zeros((NST, 128), F32)
    for d in range(OWN):
        pay[d, 0:NST, :] = state.astype(BF16)
        pay[d, NST : NST + TAIL, :] = asks[d]
        if d < OWN - 1:
            decay = decayed(got[d, NST : NST + TAIL, :])
            state = decay * state + got[d, 0:NST, :].astype(F32)


def head_weights(run_rows, run_lanes, h, lanes, mask, aff, forward):
    a = run_rows[:, h : h + 1]
    b = run_lanes[h : h + 1, lanes]
    gap = a - b if forward else b - a
    return (jnp.exp2(jnp.where(mask, gap, NEG)) * aff).astype(BF16)


def lane_masks():
    which = iota((BLK, 128), 1) >> 5
    return [(which == q).astype(F32).astype(BF16) for q in range(4)]


def group_out(run_rows, run_lanes, first, lanes, mask, aff, values, masks, forward):
    ws = [
        head_weights(run_rows, run_lanes, first + q, lanes, mask, aff, forward) for q in range(4)
    ]
    return dot(
        jnp.concatenate(ws, axis=1), jnp.concatenate([values * m for m in masks], axis=0)
    )


def fore_local_body(x, wr, rd, run, step, out, mid):
    run2 = run[...] * LOG2E
    run_lanes = run2.T
    masks = lane_masks()
    mask = iota((BLK, BLK), 0) >= iota((BLK, BLK), 1)
    base = spreader()
    step_pair = split_pair(step[...])
    edge = run2[BLK - 1 : BLK, :]
    for b in range(2):
        rows = slice(b * BLK, (b + 1) * BLK)
        run_rows = run2[rows, :]
        aff = dot_t(rd[rows, :], wr[rows, :])
        if b == 0:
            side = split_pair(step[rows, :] * jnp.exp2(edge - run_rows))
            wt = turned(wr[rows, :])
        else:
            side = split_pair(jnp.exp2(run_rows - edge))
        for c in range(NCH):
            e = spread_of(base, c)
            xs = x[rows, cols(c)].astype(F32)
            values = (xs * dot(step_pair[rows, :], e)).astype(BF16)
            sides = dot(side, e)
            if b == 0:
                mid[:, cols(c)] = dot(wt, (xs * sides).astype(BF16)).astype(BF16)
            else:
                carried = sides * dot(rd[rows, :], mid[:, cols(c)])
            for k in range(2):
                lanes = slice(k * 128, (k + 1) * 128)
                o = group_out(
                    run_rows, run_lanes, 8 * c + 4 * k, rows, mask, aff, values[:, lanes], masks, True
                )
                if b == 1:
                    o = o + carried[:, lanes]
                out[rows, c * CH + k * 128 : c * CH + (k + 1) * 128] = o


def back_local_body(og, wr, rd, run, out, mid):
    run2 = run[...] * LOG2E
    run_lanes = run2.T
    masks = lane_masks()
    mask = iota((BLK, BLK), 0) <= iota((BLK, BLK), 1)
    base = spreader()
    edge = run2[BLK - 1 : BLK, :]
    for b in (1, 0):
        rows = slice(b * BLK, (b + 1) * BLK)
        run_rows = run2[rows, :]
        aff = dot_t(wr[rows, :], rd[rows, :])
        if b == 1:
            side = split_pair(jnp.exp2(run_rows - edge))
            rt = turned(rd[rows, :])
        else:
            side = split_pair(jnp.exp2(edge - run_rows))
        for c in range(NCH):
            e = spread_of(base, c)
            values = og[rows, cols(c)]
            sides = dot(side, e)
            if b == 1:
                mid[:, cols(c)] = dot(rt, (values.astype(F32) * sides).astype(BF16)).astype(BF16)
            else:
                carried = sides * dot(wr[rows, :], mid[:, cols(c)])
            for k in range(2):
                lanes = slice(k * 128, (k + 1) * 128)
                o = group_out(
                    run_rows, run_lanes, 8 * c + 4 * k, rows, mask, aff, values[:, lanes], masks, False
                )
                if b == 0:
                    o = o + carried[:, lanes]
                out[rows, c * CH + k * 128 : c * CH + (k + 1) * 128] = o


def places_body(ids, depth, count, camera, gain, asks, place_col, place_row, live, tile_gain):
    idv = ids[...].astype(F32)
    dep = depth[...]
    seq = jnp.zeros((SLOTS, TILES), F32)
    for s in range(SLOTS):
        seq = seq + jnp.where(dep == s, idv[s : s + 1, :], 0.0)
    seq = seq.T
    live[...] = jnp.where(dep < count[...], 0.95, 0.0).T
    hot = (iota((8, TILES), 0) == camera[...]).astype(F32).T
    vg = gain[...].T
    wide = iota((8, FEAT), 1)
    gains = jnp.where(wide < 64, vg[:, 0:1], jnp.where(wide < 128, vg[:, 1:2], vg[:, 2:3]))
    per_tile = jnp.zeros((TILES, FEAT), F32)
    for v in range(8):
        per_tile = per_tile + hot[:, v : v + 1] * gains[v : v + 1, :]
    tile_gain[...] = per_tile
    lane = iota((128, 128), 1)
    lane_f = lane.astype(F32)
    below = (iota((128, 128), 0) > lane).astype(F32).astype(BF16)
    seen = jnp.zeros((1, 128), F32)
    total = jnp.zeros((128, 128), F32)
    for b in range(ROWS // 128):
        two = [jnp.broadcast_to(seq[:, k : k + 1], (TILES, 128)) for k in (2 * b, 2 * b + 1)]
        token = jnp.concatenate(two, axis=0).astype(jnp.int32)
        owner = token >> 8
        local = (token & 255).astype(F32)
        hot = owner == lane
        hot_f = hot.astype(F32)
        rank = dot(below, hot_f.astype(BF16)) + seen
        seen = seen + jnp.sum(hot_f, axis=0, keepdims=True)
        mine = jnp.sum(jnp.where(hot, rank, 0.0), axis=1, keepdims=True)
        mine = jnp.broadcast_to(mine, (128, 128))
        place = mine + (owner * 128).astype(F32)
        place_col[b * 128 : (b + 1) * 128, :] = place
        place_row[:, b * 128 : (b + 1) * 128] = place.T[0:8, :]
        named = jnp.where(hot, local, 0.0)
        total = total + dot(turned(named), (mine == lane_f).astype(F32).astype(BF16))
    first = iota((TAIL, 128), 0) == 0
    for o in range(OWN):
        asks[o] = jnp.where(first, total[o : o + 1, :], 0.0).astype(BF16)


def features_body(local, got, rd, run, weight, scan_out, answer):
    base = spreader()
    lead = split_pair(jnp.exp(run[...]))
    asked = jnp.concatenate(
        [got[d, NST : NST + TAIL, :].astype(F32)[0:1, :] for d in range(OWN)]
        + [jnp.zeros((128 - OWN, 128), F32)],
        axis=0,
    ).T
    feat = jnp.zeros((TOK, FEAT), F32)
    for c in range(NCH):
        state = jnp.concatenate([got[2 * c, 0:NST, :], got[2 * c + 1, 0:NST, :]], axis=1)
        rows = local[:, cols(c)] + dot(lead, spread_of(base, c)) * dot(rd[...], state)
        rows = rows.astype(BF16)
        scan_out[:, cols(c)] = rows
        feat = feat + dot(rows, weight[cols(c), :])
    feat = feat.astype(BF16)
    token = iota((128, TOK), 1).astype(F32)
    for d in range(OWN):
        pick = (asked[:, d : d + 1] == token).astype(F32).astype(BF16)
        answer[d] = dot(pick, feat).astype(BF16)


def composite_body(
    ans, place_col, place_row, live, tile_gain, target, out, slots, keep, trans, grads
):
    lane_f = iota((256, 128), 1).astype(F32)
    for b in range(ROWS // 256):
        rows = slice(b * 256, (b + 1) * 256)
        place = place_col[rows, :]
        hot = jnp.concatenate(
            [(place == lane_f + 128.0 * o).astype(F32).astype(BF16) for o in range(OWN)], axis=1
        )
        slots[rows, :] = dot(hot, ans[...])
    lane = iota((TILES, 128), 1)
    left = lane < GAUSS_LANES
    gain_a, gain_b = tile_gain[:, 0:128], tile_gain[:, 128:256]
    target_a = target[:, 0:128]
    target_b = jnp.concatenate([target[:, 128:192], jnp.zeros((TILES, 64), F32)], axis=1)
    t = jnp.ones((TILES, 128), F32)
    ra = jnp.zeros((TILES, 128), F32)
    rb = jnp.zeros((TILES, 128), F32)
    for k in range(SLOTS):
        rows = slice(k * TILES, (k + 1) * TILES)
        sa = jax.nn.sigmoid(slots[rows, 0:128])
        sb = jax.nn.sigmoid(slots[rows, 128:256])
        so = jnp.where(left, pltpu.roll(sb, 64, 1), sb)
        a = so * live[:, k : k + 1]
        w = t * a
        ra = ra + w * sa
        rb = rb + w * sb
        slots[rows, 0:128] = sa
        slots[rows, 128:256] = sb
        keep[rows, :] = so
        trans[rows, :] = t
        t = t * (1.0 - a)
    ea = ra * gain_a - target_a
    eb = rb * gain_b - target_b
    ga = ea * lax.rsqrt(ea * ea + 0.01) * gain_a
    gb = jnp.where(left, eb * lax.rsqrt(eb * eb + 0.01) * gain_b, 0.0)
    dt = jnp.zeros((TILES, 128), F32)
    for k in reversed(range(SLOTS)):
        rows = slice(k * TILES, (k + 1) * TILES)
        sa = slots[rows, 0:128]
        sb = slots[rows, 128:256]
        so = keep[rows, :]
        t = trans[rows, :]
        a = so * live[:, k : k + 1]
        ua = ga * sa
        ub = gb * sb
        q = ua + ub
        q = q + pltpu.roll(q, 64, 1)
        da = t * (q - dt)
        dt = a * q + (1.0 - a) * dt
        w = t * a
        grads[rows, 0:128] = (w * ua * (1.0 - sa)).astype(BF16)
        grads[rows, 128:256] = jnp.where(
            left, w * ub * (1.0 - sb), da * a * (1.0 - so)
        ).astype(BF16)
    sub_f = iota((256, ROWS), 0).astype(F32)
    place = place_row[0:1, :]
    for b in range(OWN * 128 // 256):
        hot = (place == sub_f + 256.0 * b).astype(F32).astype(BF16)
        out[b * 256 : (b + 1) * 256, :] = dot(hot, grads[...]).astype(BF16)


GAUSS_LANES = 64


def token_grad_body(homed, asked, weight, scan_out, rd, run, out_grad, pay):
    token = iota((TOK, 128), 0).astype(F32)
    hot = jnp.concatenate(
        [
            (asked[d].astype(F32)[0:1, :] == token).astype(F32).astype(BF16)
            for d in range(OWN)
        ],
        axis=1,
    )
    feat = dot(hot, homed[...])
    low = feat.astype(BF16)
    low_t = turned(low)
    base = spreader()
    lead = split_pair(jnp.exp(run[...]))
    rt = turned(rd[...])
    for c in range(NCH):
        og = dot_t(low, weight[cols(c), :]).astype(BF16)
        out_grad[:, cols(c)] = og
        scaled = (og.astype(F32) * dot(lead, spread_of(base, c))).astype(BF16)
        end = dot(rt, scaled).astype(BF16)
        part = dot(low_t, scan_out[:, cols(c)]).astype(BF16)
        for k in range(2):
            lanes = slice(k * 128, (k + 1) * 128)
            pay[2 * c + k, 0:NST, :] = end[:, lanes]
            pay[2 * c + k, NST : NST + FEAT, :] = part[:, lanes]


def suffix_body(got, tails, pay, part):
    state = jnp.zeros((NST, 128), F32)
    for d in reversed(range(OWN)):
        pay[d] = state.astype(BF16)
        if d > 0:
            state = decayed(tails[d]) * state + got[d, 0:NST, :].astype(F32)
    total = jnp.zeros((FEAT, 128), F32)
    for d in range(OWN):
        total = total + got[d, NST : NST + FEAT, :].astype(F32)
    part[...] = total


def spread_weight_body(scale, part, pay):
    block = (part[...] * scale).T.astype(BF16)
    for d in range(OWN):
        pay[d] = block


def input_grad_body(within, got, wr, run, step, grad):
    base = spreader()
    run_v = run[...]
    tail = split_pair(jnp.exp(run_v[TOK - 1 : TOK, :] - run_v))
    steps = split_pair(step[...])
    for c in range(NCH):
        e = spread_of(base, c)
        state = jnp.concatenate([got[2 * c], got[2 * c + 1]], axis=1)
        rows = within[:, cols(c)] + dot(tail, e) * dot(wr[...], state)
        grad[:, cols(c)] = (rows * dot(steps, e)).astype(BF16)


def swap(x, axes):
    return lax.all_to_all(x, axes, split_axis=0, concat_axis=0, tiled=True)


def shards(
    ssm_input,
    write_basis,
    read_basis,
    step_size,
    log_decay,
    head_weight,
    block_list,
    block_count,
    depth_order,
    camera_index,
    view_gain,
    target_color,
):
    x, wr, rd = ssm_input[0], write_basis[0], read_basis[0]
    buf = pltpu.VMEM

    pay, run, step = call(
        local_end_body,
        [((OWN, NST + TAIL, 128), BF16), ((TOK, 128), F32, 1), ((TOK, 128), F32, 1)],
        [ANY] * 4,
        [VMEM] * 3,
        scratch=[
            buf((TOK, WID), BF16),
            buf((TOK, NST), BF16),
            buf((HEADS, TOK), F32),
            buf((HEADS, TOK), F32),
            pltpu.SemaphoreType.DMA((4,)),
        ],
        flops=1 << 29,
    )(far(x), far(wr), far(step_size[0].T), far(log_decay[0].T))
    ends = swap(pay, SEQ)
    asks, place_col, place_row, live, tile_gain = call(
        places_body,
        [
            ((OWN, TAIL, 128), BF16, 1),
            ((ROWS, 128), F32, 1),
            ((8, ROWS), F32, 1),
            ((TILES, SLOTS), F32, 1),
            ((TILES, FEAT), F32, 1),
        ],
        [VMEM] * 5,
        [VMEM] * 5,
        flops=1 << 31,
    )(block_list[0].T, depth_order[0].T, block_count, camera_index, view_gain[0].T)
    (local,) = call(
        fore_local_body,
        [((TOK, WID), F32, 1)],
        [VMEM] * 5,
        [VMEM],
        scratch=[buf((NST, WID), BF16)],
        flops=1 << 32,
    )(x, wr, rd, held(run), held(step))
    (pay,) = call(
        prefix_body, [((OWN, NST + TAIL, 128), BF16)], [VMEM, VMEM], [VMEM]
    )(ends, held(asks))
    states = swap(pay, SEQ)
    scan_out, answer = call(
        features_body,
        [((TOK, WID), BF16, 1), ((OWN, 128, FEAT), BF16)],
        [VMEM] * 5,
        [VMEM] * 2,
        flops=1 << 31,
    )(held(local), states, rd, held(run), head_weight)
    answered = swap(answer, SEQ)
    (outgoing,) = call(
        composite_body,
        [((OWN * 128, FEAT), BF16)],
        [VMEM] * 6,
        [VMEM],
        scratch=[
            buf((ROWS, FEAT), F32),
            buf((ROWS, 128), F32),
            buf((ROWS, 128), F32),
            buf((ROWS, FEAT), BF16),
        ],
        flops=1 << 32,
    )(
        answered.reshape(OWN * 128, FEAT),
        held(place_col),
        held(place_row),
        held(live),
        held(tile_gain),
        target_color[0],
    )
    homed = swap(outgoing.reshape(OWN, 128, FEAT), SEQ)
    out_grad, pay = call(
        token_grad_body,
        [((TOK, WID), BF16, 1), ((OWN, NST + FEAT, 128), BF16)],
        [VMEM, TAIL_SPEC, VMEM, VMEM, VMEM, VMEM],
        [VMEM, VMEM],
        grid=(1,),
        flops=1 << 31,
    )(homed.reshape(OWN * 128, FEAT), states, head_weight, held(scan_out), rd, held(run))
    back = swap(pay, SEQ)
    (within,) = call(
        back_local_body,
        [((TOK, WID), F32, 1)],
        [VMEM] * 4,
        [VMEM],
        scratch=[buf((NST, WID), BF16)],
        flops=1 << 32,
    )(held(out_grad), wr, rd, held(run))
    pay, part = call(
        suffix_body,
        [((OWN, NST, 128), BF16), ((FEAT, 128), F32)],
        [VMEM, TAIL_SPEC],
        [VMEM, VMEM],
        grid=(1,),
    )(back, ends)
    states_back = swap(pay, SEQ)
    scenes = lax.axis_size("dp")
    hop = 1
    while hop < scenes:
        part = part + lax.ppermute(part, "dp", [(i, i ^ hop) for i in range(scenes)])
        hop *= 2
    scale = np.float32(1.0 / np.sqrt(float(scenes * TOK * lax.axis_size(SEQ))))
    (pay,) = call(
        lambda *refs: spread_weight_body(scale, *refs),
        [((OWN, 128, FEAT), BF16)],
        [VMEM],
        [VMEM],
    )(part)
    wgrad = swap(pay, SEQ).reshape(WID, FEAT).astype(F32)
    (grad,) = call(
        input_grad_body, [((TOK, WID), BF16)], [VMEM] * 5, [VMEM], flops=1 << 30
    )(held(within), states_back, wr, held(run), held(step))
    return grad[None], wgrad


def solution(mesh):
    torus = Mesh(mesh.devices.reshape(mesh.shape["dp"], 4, 4), ("dp", "seq_0", "seq_1"))
    in_specs = (
        P("dp", SEQ, None),
        P("dp", SEQ, None),
        P("dp", SEQ, None),
        P("dp", SEQ, None),
        P("dp", SEQ, None),
        P(),
        P("dp", SEQ, None),
        P("dp", SEQ),
        P("dp", SEQ, None),
        P("dp", SEQ),
        P("dp", None, None),
        P("dp", SEQ, None),
    )
    out_specs = (P("dp", SEQ, None), P())
    return jax.shard_map(
        shards, mesh=torus, in_specs=in_specs, out_specs=out_specs, check_vma=False
    )
```

```python
import jax
import jax.numpy as jnp
import numpy as np
from jax import lax
from jax.experimental import pallas as pl
from jax.experimental.pallas import tpu as pltpu
from jax.sharding import Mesh
from jax.sharding import PartitionSpec as P

SEQ = ("seq_0", "seq_1")
F32 = jnp.float32
BF16 = jnp.bfloat16
NEG = -1e30
LOG2E = 1.4426950408889634

OWN = 16
TOK = 256
BLK = 128
NST = 128
HEADS = 64
WID = 2048
FEAT = 256
CH = 256
NCH = WID // CH
TILES = 64
SLOTS = 16
ROWS = TILES * SLOTS
TAIL = 8


def dot(a, b):
    return lax.dot_general(a, b, (((1,), (0,)), ((), ())), preferred_element_type=F32)


def dot_t(a, b):
    return lax.dot_general(a, b, (((1,), (1,)), ((), ())), preferred_element_type=F32)


def iota(shape, dim):
    return lax.broadcasted_iota(jnp.int32, shape, dim)


def turned(a):
    return a.astype(F32).T.astype(BF16)


def split_pair(f):
    high = f.astype(BF16).astype(F32)
    return jnp.where(iota(f.shape, 1) < HEADS, high, f - high).astype(BF16)


def spreader():
    return (iota((2 * HEADS, CH), 0) & (HEADS - 1)) - (iota((2 * HEADS, CH), 1) >> 5)


def spread_of(base, c):
    return (base == 8 * c).astype(F32).astype(BF16)


def cols(c):
    return slice(c * CH, (c + 1) * CH)


ANY = pl.BlockSpec(memory_space=pl.ANY)
VMEM = pl.BlockSpec(memory_space=pltpu.VMEM)
SMEM = pl.BlockSpec(memory_space=pltpu.SMEM)
TAIL_SPEC = pl.BlockSpec((OWN, TAIL, 128), lambda *_: (0, NST // TAIL, 0))


PLACES = (pltpu.HBM, pltpu.VMEM)


def held(x):
    return pltpu.with_memory_space_constraint(x, pltpu.VMEM)


def far(x):
    return pltpu.with_memory_space_constraint(x, pltpu.HBM)


def call(body, outs, ins, out_specs, scratch=(), limit=16, flops=0, grid=()):
    return pl.pallas_call(
        body,
        out_shape=[
            (PLACES[o[2]] if len(o) == 3 else jax.ShapeDtypeStruct)(o[0], o[1])
            for o in outs
        ],
        grid_spec=pl.GridSpec(
            grid=grid, in_specs=ins, out_specs=out_specs, scratch_shapes=list(scratch)
        ),
        compiler_params=pltpu.CompilerParams(vmem_limit_bytes=limit << 20),
        cost_estimate=pl.CostEstimate(flops=flops, transcendentals=0, bytes_accessed=4 << 20),
    )


def local_end_body(
    core, x_far, wr_far, step_far, logd_far, pay, run_out, step_out, x, wr, step, logd, sem
):
    moves = [
        pltpu.make_async_copy(a, b, sem.at[k])
        for k, (a, b) in enumerate(
            ((logd_far, logd), (step_far, step), (wr_far, wr), (x_far, x))
        )
    ]
    del core
    for m in moves:
        m.start()
    moves[0].wait()
    moves[1].wait()
    ld = jnp.concatenate([logd[...], logd[...]], axis=0).T
    st = jnp.concatenate([step[...], step[...]], axis=0).T
    row = iota((TOK, 2 * HEADS), 0)
    run = ld
    s = 1
    while s < TOK:
        run = run + jnp.where(row >= s, pltpu.roll(run, s, 0), 0.0)
        s *= 2
    run_out[...] = run
    step_out[...] = st
    total = run[TOK - 1 : TOK, :]
    pair = split_pair(st * jnp.exp(total - run))
    t1 = total.astype(BF16).astype(F32)
    t2 = (total - t1).astype(BF16).astype(F32)
    t3 = total - t1 - t2
    trow = iota((TAIL, 2 * HEADS), 0)
    tails = jnp.where(trow == 0, t1, jnp.where(trow == 1, t2, jnp.where(trow == 2, t3, 0.0)))
    tails = jnp.where(iota((TAIL, 2 * HEADS), 1) < HEADS, tails, 0.0).astype(BF16)
    moves[2].wait()
    wt = turned(wr[...])
    base = spreader()
    moves[3].wait()
    for c in range(NCH):
        e = spread_of(base, c)
        xs = (x[:, cols(c)].astype(F32) * dot(pair, e)).astype(BF16)
        end = dot(wt, xs).astype(BF16)
        extra = dot(tails, e).astype(BF16)
        for k in range(2):
            lanes = slice(k * 128, (k + 1) * 128)
            pay[2 * c + k, 0:NST, :] = end[:, lanes]
            pay[2 * c + k, NST : NST + TAIL, :] = extra[:, lanes]


def decayed(tail):
    return jnp.exp(
        tail[0:1, :].astype(F32) + tail[1:2, :].astype(F32) + tail[2:3, :].astype(F32)
    )


def prefix_body(got, asks, local, pay):
    del local
    state = jnp.zeros((NST, 128), F32)
    for d in range(OWN):
        pay[d, 0:NST, :] = state.astype(BF16)
        pay[d, NST : NST + TAIL, :] = asks[d]
        if d < OWN - 1:
            decay = decayed(got[d, NST : NST + TAIL, :])
            state = decay * state + got[d, 0:NST, :].astype(F32)


def head_weights(run_rows, run_lanes, h, lanes, mask, aff, forward):
    a = run_rows[:, h : h + 1]
    b = run_lanes[h : h + 1, lanes]
    gap = a - b if forward else b - a
    return (jnp.exp2(jnp.where(mask, gap, NEG)) * aff).astype(BF16)


def lane_masks():
    which = iota((BLK, 128), 1) >> 5
    return [(which == q).astype(F32).astype(BF16) for q in range(4)]


def group_out(run_rows, run_lanes, first, lanes, mask, aff, values, masks, forward):
    ws = [
        head_weights(run_rows, run_lanes, first + q, lanes, mask, aff, forward) for q in range(4)
    ]
    return dot(
        jnp.concatenate(ws, axis=1), jnp.concatenate([values * m for m in masks], axis=0)
    )


def fore_local_body(x, wr, rd, run, step, out, mid):
    run2 = run[...] * LOG2E
    run_lanes = run2.T
    masks = lane_masks()
    mask = iota((BLK, BLK), 0) >= iota((BLK, BLK), 1)
    base = spreader()
    step_pair = split_pair(step[...])
    edge = run2[BLK - 1 : BLK, :]
    for b in range(2):
        rows = slice(b * BLK, (b + 1) * BLK)
        run_rows = run2[rows, :]
        aff = dot_t(rd[rows, :], wr[rows, :])
        if b == 0:
            side = split_pair(step[rows, :] * jnp.exp2(edge - run_rows))
            wt = turned(wr[rows, :])
        else:
            side = split_pair(jnp.exp2(run_rows - edge))
        for c in range(NCH):
            e = spread_of(base, c)
            xs = x[rows, cols(c)].astype(F32)
            values = (xs * dot(step_pair[rows, :], e)).astype(BF16)
            sides = dot(side, e)
            if b == 0:
                mid[:, cols(c)] = dot(wt, (xs * sides).astype(BF16)).astype(BF16)
            else:
                carried = sides * dot(rd[rows, :], mid[:, cols(c)])
            for k in range(2):
                lanes = slice(k * 128, (k + 1) * 128)
                o = group_out(
                    run_rows, run_lanes, 8 * c + 4 * k, rows, mask, aff, values[:, lanes], masks, True
                )
                if b == 1:
                    o = o + carried[:, lanes]
                out[rows, c * CH + k * 128 : c * CH + (k + 1) * 128] = o


def back_local_body(og, wr, rd, run, out, mid):
    run2 = run[...] * LOG2E
    run_lanes = run2.T
    masks = lane_masks()
    mask = iota((BLK, BLK), 0) <= iota((BLK, BLK), 1)
    base = spreader()
    edge = run2[BLK - 1 : BLK, :]
    for b in (1, 0):
        rows = slice(b * BLK, (b + 1) * BLK)
        run_rows = run2[rows, :]
        aff = dot_t(wr[rows, :], rd[rows, :])
        if b == 1:
            side = split_pair(jnp.exp2(run_rows - edge))
            rt = turned(rd[rows, :])
        else:
            side = split_pair(jnp.exp2(edge - run_rows))
        for c in range(NCH):
            e = spread_of(base, c)
            values = og[rows, cols(c)]
            sides = dot(side, e)
            if b == 1:
                mid[:, cols(c)] = dot(rt, (values.astype(F32) * sides).astype(BF16)).astype(BF16)
            else:
                carried = sides * dot(wr[rows, :], mid[:, cols(c)])
            for k in range(2):
                lanes = slice(k * 128, (k + 1) * 128)
                o = group_out(
                    run_rows, run_lanes, 8 * c + 4 * k, rows, mask, aff, values[:, lanes], masks, False
                )
                if b == 0:
                    o = o + carried[:, lanes]
                out[rows, c * CH + k * 128 : c * CH + (k + 1) * 128] = o


def places_body(ids, depth, count, camera, gain, asks, place_col, place_row, live, tile_gain):
    idv = ids[...].astype(F32)
    dep = depth[...]
    seq = jnp.zeros((SLOTS, TILES), F32)
    for s in range(SLOTS):
        seq = seq + jnp.where(dep == s, idv[s : s + 1, :], 0.0)
    seq = seq.T
    live[...] = jnp.where(dep < count[...], 0.95, 0.0).T
    hot = (iota((8, TILES), 0) == camera[...]).astype(F32).T
    vg = gain[...].T
    wide = iota((8, FEAT), 1)
    gains = jnp.where(wide < 64, vg[:, 0:1], jnp.where(wide < 128, vg[:, 1:2], vg[:, 2:3]))
    per_tile = jnp.zeros((TILES, FEAT), F32)
    for v in range(8):
        per_tile = per_tile + hot[:, v : v + 1] * gains[v : v + 1, :]
    tile_gain[...] = per_tile
    lane = iota((128, 128), 1)
    lane_f = lane.astype(F32)
    below = (iota((128, 128), 0) > lane).astype(F32).astype(BF16)
    seen = jnp.zeros((1, 128), F32)
    total = jnp.zeros((128, 128), F32)
    for b in range(ROWS // 128):
        two = [jnp.broadcast_to(seq[:, k : k + 1], (TILES, 128)) for k in (2 * b, 2 * b + 1)]
        token = jnp.concatenate(two, axis=0).astype(jnp.int32)
        owner = token >> 8
        local = (token & 255).astype(F32)
        hot = owner == lane
        hot_f = hot.astype(F32)
        rank = dot(below, hot_f.astype(BF16)) + seen
        seen = seen + jnp.sum(hot_f, axis=0, keepdims=True)
        mine = jnp.sum(jnp.where(hot, rank, 0.0), axis=1, keepdims=True)
        mine = jnp.broadcast_to(mine, (128, 128))
        place = mine + (owner * 128).astype(F32)
        place_col[b * 128 : (b + 1) * 128, :] = place
        place_row[:, b * 128 : (b + 1) * 128] = place.T[0:8, :]
        named = jnp.where(hot, local, 0.0)
        total = total + dot(turned(named), (mine == lane_f).astype(F32).astype(BF16))
    first = iota((TAIL, 128), 0) == 0
    for o in range(OWN):
        asks[o] = jnp.where(first, total[o : o + 1, :], 0.0).astype(BF16)


def features_body(local, got, rd, run, weight, scan_out, answer):
    base = spreader()
    lead = split_pair(jnp.exp(run[...]))
    asked = jnp.concatenate(
        [got[d, NST : NST + TAIL, :].astype(F32)[0:1, :] for d in range(OWN)]
        + [jnp.zeros((128 - OWN, 128), F32)],
        axis=0,
    ).T
    feat = jnp.zeros((TOK, FEAT), F32)
    for c in range(NCH):
        state = jnp.concatenate([got[2 * c, 0:NST, :], got[2 * c + 1, 0:NST, :]], axis=1)
        rows = local[:, cols(c)] + dot(lead, spread_of(base, c)) * dot(rd[...], state)
        rows = rows.astype(BF16)
        scan_out[:, cols(c)] = rows
        feat = feat + dot(rows, weight[cols(c), :])
    feat = feat.astype(BF16)
    token = iota((128, TOK), 1).astype(F32)
    for d in range(OWN):
        pick = (asked[:, d : d + 1] == token).astype(F32).astype(BF16)
        answer[d] = dot(pick, feat).astype(BF16)


def composite_body(
    ans, place_col, place_row, live, tile_gain, target, out, slots, keep, trans, grads
):
    lane_f = iota((256, 128), 1).astype(F32)
    for b in range(ROWS // 256):
        rows = slice(b * 256, (b + 1) * 256)
        place = place_col[rows, :]
        hot = jnp.concatenate(
            [(place == lane_f + 128.0 * o).astype(F32).astype(BF16) for o in range(OWN)], axis=1
        )
        slots[rows, :] = dot(hot, ans[...])
    lane = iota((TILES, 128), 1)
    left = lane < GAUSS_LANES
    gain_a, gain_b = tile_gain[:, 0:128], tile_gain[:, 128:256]
    target_a = target[:, 0:128]
    target_b = jnp.concatenate([target[:, 128:192], jnp.zeros((TILES, 64), F32)], axis=1)
    t = jnp.ones((TILES, 128), F32)
    ra = jnp.zeros((TILES, 128), F32)
    rb = jnp.zeros((TILES, 128), F32)
    for k in range(SLOTS):
        rows = slice(k * TILES, (k + 1) * TILES)
        sa = jax.nn.sigmoid(slots[rows, 0:128])
        sb = jax.nn.sigmoid(slots[rows, 128:256])
        so = jnp.where(left, pltpu.roll(sb, 64, 1), sb)
        a = so * live[:, k : k + 1]
        w = t * a
        ra = ra + w * sa
        rb = rb + w * sb
        slots[rows, 0:128] = sa
        slots[rows, 128:256] = sb
        keep[rows, :] = so
        trans[rows, :] = t
        t = t * (1.0 - a)
    ea = ra * gain_a - target_a
    eb = rb * gain_b - target_b
    ga = ea * lax.rsqrt(ea * ea + 0.01) * gain_a
    gb = jnp.where(left, eb * lax.rsqrt(eb * eb + 0.01) * gain_b, 0.0)
    dt = jnp.zeros((TILES, 128), F32)
    for k in reversed(range(SLOTS)):
        rows = slice(k * TILES, (k + 1) * TILES)
        sa = slots[rows, 0:128]
        sb = slots[rows, 128:256]
        so = keep[rows, :]
        t = trans[rows, :]
        a = so * live[:, k : k + 1]
        ua = ga * sa
        ub = gb * sb
        q = ua + ub
        q = q + pltpu.roll(q, 64, 1)
        da = t * (q - dt)
        dt = a * q + (1.0 - a) * dt
        w = t * a
        grads[rows, 0:128] = (w * ua * (1.0 - sa)).astype(BF16)
        grads[rows, 128:256] = jnp.where(
            left, w * ub * (1.0 - sb), da * a * (1.0 - so)
        ).astype(BF16)
    sub_f = iota((256, ROWS), 0).astype(F32)
    place = place_row[0:1, :]
    for b in range(OWN * 128 // 256):
        hot = (place == sub_f + 256.0 * b).astype(F32).astype(BF16)
        out[b * 256 : (b + 1) * 256, :] = dot(hot, grads[...]).astype(BF16)


GAUSS_LANES = 64
HALF = 128


def token_grad_body(homed, asked, weight, scan_out, rd, run, out_grad, pay):
    token = iota((TOK, 128), 0).astype(F32)
    hot = jnp.concatenate(
        [
            (asked[d].astype(F32)[0:1, :] == token).astype(F32).astype(BF16)
            for d in range(OWN)
        ],
        axis=1,
    )
    feat = dot(hot, homed[...])
    low = feat.astype(BF16)
    low_t = turned(low)
    base = spreader()
    lead = split_pair(jnp.exp(run[...]))
    rt = turned(rd[...])
    for c in range(NCH):
        og = dot_t(low, weight[cols(c), :]).astype(BF16)
        out_grad[:, cols(c)] = og
        scaled = (og.astype(F32) * dot(lead, spread_of(base, c))).astype(BF16)
        end = dot(rt, scaled).astype(BF16)
        part = dot(low_t, scan_out[:, cols(c)]).astype(BF16)
        for k in range(2):
            lanes = slice(k * 128, (k + 1) * 128)
            pay[2 * c + k, 0:NST, :] = end[:, lanes]
            pay[2 * c + k, NST : NST + FEAT, :] = part[:, lanes]


def scene_sum_body(core, got, mine, theirs):
    total = jnp.zeros((FEAT, 128), F32)
    for d in range(OWN):
        total = total + got[d, NST : NST + FEAT, :].astype(F32)
    first = core[0] == 0
    mine[...] = jnp.where(first, total[0:HALF, :], total[HALF:FEAT, :])
    theirs[...] = jnp.where(first, total[HALF:FEAT, :], total[0:HALF, :])


def suffix_body(scale, got, tails, part, within, pay):
    del within
    state = jnp.zeros((NST, 128), F32)
    block = (part[...] * scale).T.astype(BF16)
    for d in reversed(range(OWN)):
        pay[d, 0:NST, :] = state.astype(BF16)
        pay[d, NST : NST + HALF, :] = block
        if d > 0:
            state = decayed(tails[d]) * state + got[d].astype(F32)


def join_weight_body(core, own, other, out):
    first = core[0] == 0
    for d in range(OWN):
        rows = slice(d * 128, (d + 1) * 128)
        a, b = own[d, NST : NST + HALF, :].astype(F32), other[d].astype(F32)
        out[rows, 0:HALF] = jnp.where(first, a, b)
        out[rows, HALF:FEAT] = jnp.where(first, b, a)


def input_grad_body(within, got, wr, run, step, grad):
    base = spreader()
    run_v = run[...]
    tail = split_pair(jnp.exp(run_v[TOK - 1 : TOK, :] - run_v))
    steps = split_pair(step[...])
    for c in range(NCH):
        e = spread_of(base, c)
        state = jnp.concatenate([got[2 * c, 0:NST, :], got[2 * c + 1, 0:NST, :]], axis=1)
        rows = within[:, cols(c)] + dot(tail, e) * dot(wr[...], state)
        grad[:, cols(c)] = (rows * dot(steps, e)).astype(BF16)


def swap(x, axes):
    return lax.all_to_all(x, axes, split_axis=0, concat_axis=0, tiled=True)


def shards(
    ssm_input,
    write_basis,
    read_basis,
    step_size,
    log_decay,
    head_weight,
    block_list,
    block_count,
    depth_order,
    camera_index,
    view_gain,
    target_color,
):
    x, wr, rd = ssm_input[0], write_basis[0], read_basis[0]
    buf = pltpu.VMEM
    scenes = lax.axis_size("dp")
    core = lax.axis_index("dp") % 2
    core_ref = core.astype(jnp.int32).reshape(1)

    def trade(v, hop):
        return lax.ppermute(v, "dp", [(i, i ^ hop) for i in range(scenes)])

    pay, run, step = call(
        local_end_body,
        [((OWN, NST + TAIL, 128), BF16), ((TOK, 128), F32, 1), ((TOK, 128), F32, 1)],
        [SMEM] + [ANY] * 4,
        [VMEM] * 3,
        scratch=[
            buf((TOK, WID), BF16),
            buf((TOK, NST), BF16),
            buf((HEADS, TOK), F32),
            buf((HEADS, TOK), F32),
            pltpu.SemaphoreType.DMA((4,)),
        ],
        flops=1 << 29,
    )(core_ref, far(x), far(wr), far(step_size[0].T), far(log_decay[0].T))
    ends = swap(pay, SEQ)
    asks, place_col, place_row, live, tile_gain = call(
        places_body,
        [
            ((OWN, TAIL, 128), BF16, 1),
            ((ROWS, 128), F32, 0),
            ((8, ROWS), F32, 0),
            ((TILES, SLOTS), F32, 0),
            ((TILES, FEAT), F32, 0),
        ],
        [VMEM] * 5,
        [VMEM] * 5,
        flops=1 << 31,
    )(block_list[0].T, depth_order[0].T, block_count, camera_index, view_gain[0].T)
    (local,) = call(
        fore_local_body,
        [((TOK, WID), F32, 0)],
        [VMEM] * 5,
        [VMEM],
        scratch=[buf((NST, WID), BF16)],
        flops=1 << 32,
    )(x, wr, rd, held(run), held(step))
    (pay,) = call(
        prefix_body, [((OWN, NST + TAIL, 128), BF16)], [VMEM, VMEM, ANY], [VMEM]
    )(ends, held(asks), far(local))
    states = swap(pay, SEQ)
    scan_out, answer = call(
        features_body,
        [((TOK, WID), BF16, 1), ((OWN, 128, FEAT), BF16)],
        [VMEM] * 5,
        [VMEM] * 2,
        flops=1 << 31,
    )(local, states, rd, held(run), head_weight)
    answered = swap(answer, SEQ)
    (outgoing,) = call(
        composite_body,
        [((OWN * 128, FEAT), BF16)],
        [VMEM] * 6,
        [VMEM],
        scratch=[
            buf((ROWS, FEAT), F32),
            buf((ROWS, 128), F32),
            buf((ROWS, 128), F32),
            buf((ROWS, FEAT), BF16),
        ],
        flops=1 << 32,
    )(
        answered.reshape(OWN * 128, FEAT),
        place_col,
        place_row,
        live,
        tile_gain,
        target_color[0],
    )
    homed = swap(outgoing.reshape(OWN, 128, FEAT), SEQ)
    out_grad, pay = call(
        token_grad_body,
        [((TOK, WID), BF16, 1), ((OWN, NST + FEAT, 128), BF16)],
        [VMEM, TAIL_SPEC, VMEM, VMEM, VMEM, VMEM],
        [VMEM, VMEM],
        grid=(1,),
        flops=1 << 31,
    )(homed.reshape(OWN * 128, FEAT), states, head_weight, held(scan_out), rd, held(run))
    back = swap(pay, SEQ)
    (within,) = call(
        back_local_body,
        [((TOK, WID), F32, 1)],
        [VMEM] * 4,
        [VMEM],
        scratch=[buf((NST, WID), BF16)],
        flops=1 << 32,
    )(held(out_grad), wr, rd, held(run))
    mine, theirs = call(
        scene_sum_body, [((HALF, 128), F32)] * 2, [SMEM, VMEM], [VMEM] * 2
    )(core_ref, back)
    part = mine + trade(theirs, 1)
    hop = 2
    while hop < scenes:
        part = part + trade(part, hop)
        hop *= 2
    scale = np.float32(1.0 / np.sqrt(float(scenes * TOK * lax.axis_size(SEQ))))
    (pay,) = call(
        lambda *refs: suffix_body(scale, *refs),
        [((OWN, NST + HALF, 128), BF16)],
        [pl.BlockSpec((OWN, NST, 128), lambda *_: (0, 0, 0)), TAIL_SPEC, VMEM, ANY],
        [VMEM],
        grid=(1,),
    )(back, ends, part, within)
    last = swap(pay, SEQ)
    other = trade(last[:, NST:, :], 1)
    (grad,) = call(
        input_grad_body, [((TOK, WID), BF16)], [VMEM] * 5, [VMEM], flops=1 << 30
    )(held(within), last, wr, held(run), held(step))
    (wgrad,) = call(
        join_weight_body, [((WID, FEAT), F32)], [SMEM, VMEM, VMEM], [VMEM]
    )(core_ref, last, other)
    return grad[None], wgrad


def solution(mesh):
    torus = Mesh(mesh.devices.reshape(mesh.shape["dp"], 4, 4), ("dp", "seq_0", "seq_1"))
    in_specs = (
        P("dp", SEQ, None),
        P("dp", SEQ, None),
        P("dp", SEQ, None),
        P("dp", SEQ, None),
        P("dp", SEQ, None),
        P(),
        P("dp", SEQ, None),
        P("dp", SEQ),
        P("dp", SEQ, None),
        P("dp", SEQ),
        P("dp", None, None),
        P("dp", SEQ, None),
    )
    out_specs = (P("dp", SEQ, None), P())
    return jax.shard_map(
        shards, mesh=torus, in_specs=in_specs, out_specs=out_specs, check_vma=False
    )
```

```python
import jax
import jax.numpy as jnp
import numpy as np
from jax import lax
from jax.experimental import pallas as pl
from jax.experimental.pallas import tpu as pltpu
from jax.sharding import Mesh
from jax.sharding import PartitionSpec as P

SEQ = ("seq_0", "seq_1")
F32 = jnp.float32
BF16 = jnp.bfloat16
NEG = -1e30
LOG2E = 1.4426950408889634

OWN = 16
TOK = 256
BLK = 128
NST = 128
HEADS = 64
WID = 2048
FEAT = 256
CH = 256
NCH = WID // CH
TILES = 64
SLOTS = 16
ROWS = TILES * SLOTS
TAIL = 8


def dot(a, b):
    return lax.dot_general(a, b, (((1,), (0,)), ((), ())), preferred_element_type=F32)


def dot_t(a, b):
    return lax.dot_general(a, b, (((1,), (1,)), ((), ())), preferred_element_type=F32)


def iota(shape, dim):
    return lax.broadcasted_iota(jnp.int32, shape, dim)


def turned(a):
    return a.astype(F32).T.astype(BF16)


def split_pair(f):
    high = f.astype(BF16).astype(F32)
    return jnp.where(iota(f.shape, 1) < HEADS, high, f - high).astype(BF16)


def spreader():
    return (iota((2 * HEADS, CH), 0) & (HEADS - 1)) - (iota((2 * HEADS, CH), 1) >> 5)


def spread_of(base, c):
    return (base == 8 * c).astype(F32).astype(BF16)


def cols(c):
    return slice(c * CH, (c + 1) * CH)


ANY = pl.BlockSpec(memory_space=pl.ANY)
VMEM = pl.BlockSpec(memory_space=pltpu.VMEM)
SMEM = pl.BlockSpec(memory_space=pltpu.SMEM)
TAIL_SPEC = pl.BlockSpec((OWN, TAIL, 128), lambda *_: (0, NST // TAIL, 0))


PLACES = (pltpu.HBM, pltpu.VMEM)


def held(x):
    return pltpu.with_memory_space_constraint(x, pltpu.VMEM)


def far(x):
    return pltpu.with_memory_space_constraint(x, pltpu.HBM)


def call(body, outs, ins, out_specs, scratch=(), limit=16, flops=0, grid=()):
    return pl.pallas_call(
        body,
        out_shape=[
            (PLACES[o[2]] if len(o) == 3 else jax.ShapeDtypeStruct)(o[0], o[1])
            for o in outs
        ],
        grid_spec=pl.GridSpec(
            grid=grid, in_specs=ins, out_specs=out_specs, scratch_shapes=list(scratch)
        ),
        compiler_params=pltpu.CompilerParams(vmem_limit_bytes=limit << 20),
        cost_estimate=pl.CostEstimate(flops=flops, transcendentals=0, bytes_accessed=4 << 20),
    )


def local_end_body(
    core, x_far, wr_far, step_far, logd_far, pay, run_out, step_out, x, wr, step, logd, sem
):
    moves = [
        pltpu.make_async_copy(a, b, sem.at[k])
        for k, (a, b) in enumerate(
            ((logd_far, logd), (step_far, step), (wr_far, wr), (x_far, x))
        )
    ]
    del core
    for m in moves:
        m.start()
    moves[0].wait()
    moves[1].wait()
    ld = jnp.concatenate([logd[...], logd[...]], axis=0).T
    st = jnp.concatenate([step[...], step[...]], axis=0).T
    row = iota((TOK, 2 * HEADS), 0)
    run = ld
    s = 1
    while s < TOK:
        run = run + jnp.where(row >= s, pltpu.roll(run, s, 0), 0.0)
        s *= 2
    run_out[...] = run
    step_out[...] = st
    total = run[TOK - 1 : TOK, :]
    pair = split_pair(st * jnp.exp(total - run))
    t1 = total.astype(BF16).astype(F32)
    t2 = (total - t1).astype(BF16).astype(F32)
    t3 = total - t1 - t2
    trow = iota((TAIL, 2 * HEADS), 0)
    tails = jnp.where(trow == 0, t1, jnp.where(trow == 1, t2, jnp.where(trow == 2, t3, 0.0)))
    tails = jnp.where(iota((TAIL, 2 * HEADS), 1) < HEADS, tails, 0.0).astype(BF16)
    moves[2].wait()
    wt = turned(wr[...])
    base = spreader()
    moves[3].wait()
    for c in range(NCH):
        e = spread_of(base, c)
        xs = (x[:, cols(c)].astype(F32) * dot(pair, e)).astype(BF16)
        end = dot(wt, xs).astype(BF16)
        extra = dot(tails, e).astype(BF16)
        for k in range(2):
            lanes = slice(k * 128, (k + 1) * 128)
            pay[2 * c + k, 0:NST, :] = end[:, lanes]
            pay[2 * c + k, NST : NST + TAIL, :] = extra[:, lanes]


def decayed(tail):
    return jnp.exp(
        tail[0:1, :].astype(F32) + tail[1:2, :].astype(F32) + tail[2:3, :].astype(F32)
    )


def prefix_body(got, asks, local, pay):
    del local
    state = jnp.zeros((NST, 128), F32)
    for d in range(OWN):
        pay[d, 0:NST, :] = state.astype(BF16)
        pay[d, NST : NST + TAIL, :] = asks[d]
        if d < OWN - 1:
            decay = decayed(got[d, NST : NST + TAIL, :])
            state = decay * state + got[d, 0:NST, :].astype(F32)


def head_weights(run_rows, run_lanes, h, lanes, mask, aff, forward):
    a = run_rows[:, h : h + 1]
    b = run_lanes[h : h + 1, lanes]
    gap = a - b if forward else b - a
    return (jnp.exp2(jnp.where(mask, gap, NEG)) * aff).astype(BF16)


def lane_masks():
    which = iota((BLK, 128), 1) >> 5
    return [(which == q).astype(F32).astype(BF16) for q in range(4)]


def group_out(run_rows, run_lanes, first, lanes, mask, aff, values, masks, forward):
    ws = [
        head_weights(run_rows, run_lanes, first + q, lanes, mask, aff, forward) for q in range(4)
    ]
    return dot(
        jnp.concatenate(ws, axis=1), jnp.concatenate([values * m for m in masks], axis=0)
    )


def fore_local_body(x, wr, rd, run, step, out, mid):
    run2 = run[...] * LOG2E
    run_lanes = run2.T
    masks = lane_masks()
    mask = iota((BLK, BLK), 0) >= iota((BLK, BLK), 1)
    base = spreader()
    step_pair = split_pair(step[...])
    edge = run2[BLK - 1 : BLK, :]
    for b in range(2):
        rows = slice(b * BLK, (b + 1) * BLK)
        run_rows = run2[rows, :]
        aff = dot_t(rd[rows, :], wr[rows, :])
        if b == 0:
            side = split_pair(step[rows, :] * jnp.exp2(edge - run_rows))
            wt = turned(wr[rows, :])
        else:
            side = split_pair(jnp.exp2(run_rows - edge))
        for c in range(NCH):
            e = spread_of(base, c)
            xs = x[rows, cols(c)].astype(F32)
            values = (xs * dot(step_pair[rows, :], e)).astype(BF16)
            sides = dot(side, e)
            if b == 0:
                mid[:, cols(c)] = dot(wt, (xs * sides).astype(BF16)).astype(BF16)
            else:
                carried = sides * dot(rd[rows, :], mid[:, cols(c)])
            for k in range(2):
                lanes = slice(k * 128, (k + 1) * 128)
                o = group_out(
                    run_rows, run_lanes, 8 * c + 4 * k, rows, mask, aff, values[:, lanes], masks, True
                )
                if b == 1:
                    o = o + carried[:, lanes]
                out[rows, c * CH + k * 128 : c * CH + (k + 1) * 128] = o


def back_local_body(og, wr, rd, run, out, mid):
    run2 = run[...] * LOG2E
    run_lanes = run2.T
    masks = lane_masks()
    mask = iota((BLK, BLK), 0) <= iota((BLK, BLK), 1)
    base = spreader()
    edge = run2[BLK - 1 : BLK, :]
    for b in (1, 0):
        rows = slice(b * BLK, (b + 1) * BLK)
        run_rows = run2[rows, :]
        aff = dot_t(wr[rows, :], rd[rows, :])
        if b == 1:
            side = split_pair(jnp.exp2(run_rows - edge))
            rt = turned(rd[rows, :])
        else:
            side = split_pair(jnp.exp2(edge - run_rows))
        for c in range(NCH):
            e = spread_of(base, c)
            values = og[rows, cols(c)]
            sides = dot(side, e)
            if b == 1:
                mid[:, cols(c)] = dot(rt, (values.astype(F32) * sides).astype(BF16)).astype(BF16)
            else:
                carried = sides * dot(wr[rows, :], mid[:, cols(c)])
            for k in range(2):
                lanes = slice(k * 128, (k + 1) * 128)
                o = group_out(
                    run_rows, run_lanes, 8 * c + 4 * k, rows, mask, aff, values[:, lanes], masks, False
                )
                if b == 0:
                    o = o + carried[:, lanes]
                out[rows, c * CH + k * 128 : c * CH + (k + 1) * 128] = o


def places_body(ids, depth, count, camera, gain, asks, place_col, place_row, live, tile_gain):
    idv = ids[...].astype(F32)
    dep = depth[...]
    seq = jnp.zeros((SLOTS, TILES), F32)
    for s in range(SLOTS):
        seq = seq + jnp.where(dep == s, idv[s : s + 1, :], 0.0)
    seq = seq.T
    live[...] = jnp.where(dep < count[...], 0.95, 0.0).T
    hot = (iota((8, TILES), 0) == camera[...]).astype(F32).T
    vg = gain[...].T
    wide = iota((8, FEAT), 1)
    gains = jnp.where(wide < 64, vg[:, 0:1], jnp.where(wide < 128, vg[:, 1:2], vg[:, 2:3]))
    per_tile = jnp.zeros((TILES, FEAT), F32)
    for v in range(8):
        per_tile = per_tile + hot[:, v : v + 1] * gains[v : v + 1, :]
    tile_gain[...] = per_tile
    lane = iota((128, 128), 1)
    lane_f = lane.astype(F32)
    below = (iota((128, 128), 0) > lane).astype(F32).astype(BF16)
    seen = jnp.zeros((1, 128), F32)
    total = jnp.zeros((128, 128), F32)
    for b in range(ROWS // 128):
        two = [jnp.broadcast_to(seq[:, k : k + 1], (TILES, 128)) for k in (2 * b, 2 * b + 1)]
        token = jnp.concatenate(two, axis=0).astype(jnp.int32)
        owner = token >> 8
        local = (token & 255).astype(F32)
        hot = owner == lane
        hot_f = hot.astype(F32)
        rank = dot(below, hot_f.astype(BF16)) + seen
        seen = seen + jnp.sum(hot_f, axis=0, keepdims=True)
        mine = jnp.sum(jnp.where(hot, rank, 0.0), axis=1, keepdims=True)
        mine = jnp.broadcast_to(mine, (128, 128))
        place = mine + (owner * 128).astype(F32)
        place_col[b * 128 : (b + 1) * 128, :] = place
        place_row[:, b * 128 : (b + 1) * 128] = place.T[0:8, :]
        named = jnp.where(hot, local, 0.0)
        total = total + dot(turned(named), (mine == lane_f).astype(F32).astype(BF16))
    first = iota((TAIL, 128), 0) == 0
    for o in range(OWN):
        asks[o] = jnp.where(first, total[o : o + 1, :], 0.0).astype(BF16)


def features_body(local, got, rd, run, weight, scan_out, answer):
    base = spreader()
    lead = split_pair(jnp.exp(run[...]))
    asked = jnp.concatenate(
        [got[d, NST : NST + TAIL, :].astype(F32)[0:1, :] for d in range(OWN)]
        + [jnp.zeros((128 - OWN, 128), F32)],
        axis=0,
    ).T
    feat = jnp.zeros((TOK, FEAT), F32)
    for c in range(NCH):
        state = jnp.concatenate([got[2 * c, 0:NST, :], got[2 * c + 1, 0:NST, :]], axis=1)
        rows = local[:, cols(c)] + dot(lead, spread_of(base, c)) * dot(rd[...], state)
        rows = rows.astype(BF16)
        scan_out[:, cols(c)] = rows
        feat = feat + dot(rows, weight[cols(c), :])
    feat = feat.astype(BF16)
    token = iota((128, TOK), 1).astype(F32)
    for d in range(OWN):
        pick = (asked[:, d : d + 1] == token).astype(F32).astype(BF16)
        answer[d] = dot(pick, feat).astype(BF16)


def composite_body(
    ans, place_col, place_row, live, tile_gain, target, out, slots, keep, trans, grads
):
    one, zero = jnp.ones((256, 128), BF16), jnp.zeros((256, 128), BF16)
    lane_o = iota((256, 128), 1).astype(jnp.int16)
    for b in range(ROWS // 256):
        rows = slice(b * 256, (b + 1) * 256)
        place = place_col[rows, :].astype(jnp.int32).astype(jnp.int16)
        hot = jnp.concatenate(
            [jnp.where(place == lane_o + np.int16(128 * o), one, zero) for o in range(OWN)], axis=1
        )
        slots[rows, :] = dot(hot, ans[...])
    lane = iota((TILES, 128), 1)
    left = lane < GAUSS_LANES
    gain_a, gain_b = tile_gain[:, 0:128], tile_gain[:, 128:256]
    target_a = target[:, 0:128]
    target_b = jnp.concatenate([target[:, 128:192], jnp.zeros((TILES, 64), F32)], axis=1)
    t = jnp.ones((TILES, 128), F32)
    ra = jnp.zeros((TILES, 128), F32)
    rb = jnp.zeros((TILES, 128), F32)
    for k in range(SLOTS):
        rows = slice(k * TILES, (k + 1) * TILES)
        sa = jax.nn.sigmoid(slots[rows, 0:128])
        sb = jax.nn.sigmoid(slots[rows, 128:256])
        so = jnp.where(left, pltpu.roll(sb, 64, 1), sb)
        a = so * live[:, k : k + 1]
        w = t * a
        ra = ra + w * sa
        rb = rb + w * sb
        slots[rows, 0:128] = sa
        slots[rows, 128:256] = sb
        keep[rows, :] = so
        trans[rows, :] = t
        t = t * (1.0 - a)
    ea = ra * gain_a - target_a
    eb = rb * gain_b - target_b
    ga = ea * lax.rsqrt(ea * ea + 0.01) * gain_a
    gb = jnp.where(left, eb * lax.rsqrt(eb * eb + 0.01) * gain_b, 0.0)
    dt = jnp.zeros((TILES, 128), F32)
    for k in reversed(range(SLOTS)):
        rows = slice(k * TILES, (k + 1) * TILES)
        sa = slots[rows, 0:128]
        sb = slots[rows, 128:256]
        so = keep[rows, :]
        t = trans[rows, :]
        a = so * live[:, k : k + 1]
        ua = ga * sa
        ub = gb * sb
        q = ua + ub
        q = q + pltpu.roll(q, 64, 1)
        da = t * (q - dt)
        dt = a * q + (1.0 - a) * dt
        w = t * a
        grads[rows, 0:128] = (w * ua * (1.0 - sa)).astype(BF16)
        grads[rows, 128:256] = jnp.where(
            left, w * ub * (1.0 - sb), da * a * (1.0 - so)
        ).astype(BF16)
    sub_f = iota((256, ROWS), 0).astype(F32)
    place = place_row[0:1, :]
    for b in range(OWN * 128 // 256):
        hot = (place == sub_f + 256.0 * b).astype(F32).astype(BF16)
        out[b * 256 : (b + 1) * 256, :] = dot(hot, grads[...]).astype(BF16)


GAUSS_LANES = 64
HALF = 128


def token_grad_body(core, homed, asked, scan_out, low_out, mine, theirs):
    token = iota((TOK, 128), 0).astype(F32)
    hot = jnp.concatenate(
        [
            (asked[d].astype(F32)[0:1, :] == token).astype(F32).astype(BF16)
            for d in range(OWN)
        ],
        axis=1,
    )
    low = dot(hot, homed[...]).astype(BF16)
    low_out[...] = low
    low_t = turned(low)
    first = core[0] == 0
    upper, lower = low_t[0:HALF, :].astype(F32), low_t[HALF:FEAT, :].astype(F32)
    own = jnp.where(first, upper, lower).astype(BF16)
    far = jnp.where(first, lower, upper).astype(BF16)
    for c in range(NCH):
        for rows, out in ((far, theirs), (own, mine)):
            piece = dot(rows, scan_out[:, cols(c)]).astype(BF16)
            for k in range(2):
                out[2 * c + k] = piece[:, k * 128 : (k + 1) * 128]


def out_grad_body(low, weight, rd, run, out_grad, ends):
    base = spreader()
    lead = split_pair(jnp.exp(run[...]))
    rt = turned(rd[...])
    for c in range(NCH):
        og = dot_t(low[...], weight[cols(c), :]).astype(BF16)
        out_grad[:, cols(c)] = og
        scaled = (og.astype(F32) * dot(lead, spread_of(base, c))).astype(BF16)
        end = dot(rt, scaled).astype(BF16)
        for k in range(2):
            ends[2 * c + k] = end[:, k * 128 : (k + 1) * 128]


def join_body(ends, mine, other, pay):
    for g in range(OWN):
        pay[g, 0:NST, :] = ends[g]
        pay[g, NST : NST + HALF, :] = (mine[g].astype(F32) + other[g].astype(F32)).astype(BF16)


def scene_sum_body(got, part):
    total = jnp.zeros((HALF, 128), F32)
    for d in range(OWN):
        total = total + got[d, NST : NST + HALF, :].astype(F32)
    part[...] = total


def suffix_body(scale, got, tails, part, within, pay):
    del within
    state = jnp.zeros((NST, 128), F32)
    block = (part[...] * scale).T.astype(BF16)
    for d in reversed(range(OWN)):
        pay[d, 0:NST, :] = state.astype(BF16)
        pay[d, NST : NST + HALF, :] = block
        if d > 0:
            state = decayed(tails[d]) * state + got[d].astype(F32)


def join_weight_body(core, own, other, out):
    first = core[0] == 0
    for d in range(OWN):
        rows = slice(d * 128, (d + 1) * 128)
        a, b = own[d, NST : NST + HALF, :].astype(F32), other[d].astype(F32)
        out[rows, 0:HALF] = jnp.where(first, a, b)
        out[rows, HALF:FEAT] = jnp.where(first, b, a)


def input_grad_body(within, got, wr, run, step, grad):
    base = spreader()
    run_v = run[...]
    tail = split_pair(jnp.exp(run_v[TOK - 1 : TOK, :] - run_v))
    steps = split_pair(step[...])
    for c in range(NCH):
        e = spread_of(base, c)
        state = jnp.concatenate([got[2 * c, 0:NST, :], got[2 * c + 1, 0:NST, :]], axis=1)
        rows = within[:, cols(c)] + dot(tail, e) * dot(wr[...], state)
        grad[:, cols(c)] = (rows * dot(steps, e)).astype(BF16)


def swap(x, axes):
    return lax.all_to_all(x, axes, split_axis=0, concat_axis=0, tiled=True)


def shards(
    ssm_input,
    write_basis,
    read_basis,
    step_size,
    log_decay,
    head_weight,
    block_list,
    block_count,
    depth_order,
    camera_index,
    view_gain,
    target_color,
):
    x, wr, rd = ssm_input[0], write_basis[0], read_basis[0]
    buf = pltpu.VMEM
    scenes = lax.axis_size("dp")
    core = lax.axis_index("dp") % 2
    core_ref = core.astype(jnp.int32).reshape(1)

    def trade(v, hop):
        return lax.ppermute(v, "dp", [(i, i ^ hop) for i in range(scenes)])

    pay, run, step = call(
        local_end_body,
        [((OWN, NST + TAIL, 128), BF16), ((TOK, 128), F32, 1), ((TOK, 128), F32, 1)],
        [SMEM] + [ANY] * 4,
        [VMEM] * 3,
        scratch=[
            buf((TOK, WID), BF16),
            buf((TOK, NST), BF16),
            buf((HEADS, TOK), F32),
            buf((HEADS, TOK), F32),
            pltpu.SemaphoreType.DMA((4,)),
        ],
        flops=1 << 29,
    )(core_ref, far(x), far(wr), far(step_size[0].T), far(log_decay[0].T))
    ends = swap(pay, SEQ)
    asks, place_col, place_row, live, tile_gain = call(
        places_body,
        [
            ((OWN, TAIL, 128), BF16, 1),
            ((ROWS, 128), F32, 0),
            ((8, ROWS), F32, 0),
            ((TILES, SLOTS), F32, 0),
            ((TILES, FEAT), F32, 0),
        ],
        [VMEM] * 5,
        [VMEM] * 5,
        flops=1 << 31,
    )(block_list[0].T, depth_order[0].T, block_count, camera_index, view_gain[0].T)
    (local,) = call(
        fore_local_body,
        [((TOK, WID), F32, 0)],
        [VMEM] * 5,
        [VMEM],
        scratch=[buf((NST, WID), BF16)],
        flops=1 << 32,
    )(x, wr, rd, held(run), held(step))
    (pay,) = call(
        prefix_body, [((OWN, NST + TAIL, 128), BF16)], [VMEM, VMEM, ANY], [VMEM]
    )(ends, held(asks), far(local))
    states = swap(pay, SEQ)
    scan_out, answer = call(
        features_body,
        [((TOK, WID), BF16, 1), ((OWN, 128, FEAT), BF16)],
        [VMEM] * 5,
        [VMEM] * 2,
        flops=1 << 31,
    )(local, states, rd, held(run), head_weight)
    answered = swap(answer, SEQ)
    (outgoing,) = call(
        composite_body,
        [((OWN * 128, FEAT), BF16)],
        [VMEM] * 6,
        [VMEM],
        scratch=[
            buf((ROWS, FEAT), F32),
            buf((ROWS, 128), F32),
            buf((ROWS, 128), F32),
            buf((ROWS, FEAT), BF16),
        ],
        flops=1 << 32,
    )(
        answered.reshape(OWN * 128, FEAT),
        place_col,
        place_row,
        live,
        tile_gain,
        target_color[0],
    )
    homed = swap(outgoing.reshape(OWN, 128, FEAT), SEQ)
    low, mine, theirs = call(
        token_grad_body,
        [((TOK, FEAT), BF16, 1), ((OWN, HALF, 128), BF16), ((OWN, HALF, 128), BF16)],
        [SMEM, VMEM, TAIL_SPEC, VMEM],
        [VMEM] * 3,
        grid=(1,),
        flops=1 << 31,
    )(core_ref, homed.reshape(OWN * 128, FEAT), states, held(scan_out))
    other = trade(theirs, 1)
    out_grad, back_ends = call(
        out_grad_body,
        [((TOK, WID), BF16, 1), ((OWN, NST, 128), BF16, 1)],
        [VMEM] * 4,
        [VMEM, VMEM],
        flops=1 << 31,
    )(held(low), head_weight, rd, held(run))
    (pay,) = call(
        join_body, [((OWN, NST + HALF, 128), BF16)], [VMEM] * 3, [VMEM]
    )(held(back_ends), mine, other)
    back = swap(pay, SEQ)
    (within,) = call(
        back_local_body,
        [((TOK, WID), F32, 1)],
        [VMEM] * 4,
        [VMEM],
        scratch=[buf((NST, WID), BF16)],
        flops=1 << 32,
    )(held(out_grad), wr, rd, held(run))
    (part,) = call(scene_sum_body, [((HALF, 128), F32)], [VMEM], [VMEM])(back)
    part = (part + trade(part, 2)) + (trade(part, 4) + trade(part, 6))
    scale = np.float32(1.0 / np.sqrt(float(scenes * TOK * lax.axis_size(SEQ))))
    (pay,) = call(
        lambda *refs: suffix_body(scale, *refs),
        [((OWN, NST + HALF, 128), BF16)],
        [pl.BlockSpec((OWN, NST, 128), lambda *_: (0, 0, 0)), TAIL_SPEC, VMEM, ANY],
        [VMEM],
        grid=(1,),
    )(back, ends, part, within)
    last = swap(pay, SEQ)
    other = trade(last[:, NST:, :], 1)
    (grad,) = call(
        input_grad_body, [((TOK, WID), BF16)], [VMEM] * 5, [VMEM], flops=1 << 30
    )(held(within), last, wr, held(run), held(step))
    (wgrad,) = call(
        join_weight_body, [((WID, FEAT), F32)], [SMEM, VMEM, VMEM], [VMEM]
    )(core_ref, last, other)
    return grad[None], wgrad


def solution(mesh):
    torus = Mesh(mesh.devices.reshape(mesh.shape["dp"], 4, 4), ("dp", "seq_0", "seq_1"))
    in_specs = (
        P("dp", SEQ, None),
        P("dp", SEQ, None),
        P("dp", SEQ, None),
        P("dp", SEQ, None),
        P("dp", SEQ, None),
        P(),
        P("dp", SEQ, None),
        P("dp", SEQ),
        P("dp", SEQ, None),
        P("dp", SEQ),
        P("dp", None, None),
        P("dp", SEQ, None),
    )
    out_specs = (P("dp", SEQ, None), P())
    return jax.shard_map(
        shards, mesh=torus, in_specs=in_specs, out_specs=out_specs, check_vma=False
    )
```

```python
import jax
import jax.numpy as jnp
import numpy as np
from jax import lax
from jax.experimental import pallas as pl
from jax.experimental.pallas import tpu as pltpu
from jax.sharding import Mesh
from jax.sharding import PartitionSpec as P

SEQ = ("seq_0", "seq_1")
F32 = jnp.float32
BF16 = jnp.bfloat16
NEG = -1e30
LOG2E = 1.4426950408889634

OWN = 16
TOK = 256
BLK = 128
NST = 128
HEADS = 64
WID = 2048
FEAT = 256
CH = 256
NCH = WID // CH
TILES = 64
SLOTS = 16
ROWS = TILES * SLOTS
TAIL = 8


def dot(a, b):
    return lax.dot_general(a, b, (((1,), (0,)), ((), ())), preferred_element_type=F32)


def dot_t(a, b):
    return lax.dot_general(a, b, (((1,), (1,)), ((), ())), preferred_element_type=F32)


def iota(shape, dim):
    return lax.broadcasted_iota(jnp.int32, shape, dim)


def turned(a):
    return a.astype(F32).T.astype(BF16)


def split_pair(f):
    high = f.astype(BF16).astype(F32)
    return jnp.where(iota(f.shape, 1) < HEADS, high, f - high).astype(BF16)


def spreader():
    return (iota((2 * HEADS, CH), 0) & (HEADS - 1)) - (iota((2 * HEADS, CH), 1) >> 5)


def spread_of(base, c):
    return (base == 8 * c).astype(F32).astype(BF16)


def cols(c):
    return slice(c * CH, (c + 1) * CH)


ANY = pl.BlockSpec(memory_space=pl.ANY)
VMEM = pl.BlockSpec(memory_space=pltpu.VMEM)
SMEM = pl.BlockSpec(memory_space=pltpu.SMEM)
TAIL_SPEC = pl.BlockSpec((OWN, TAIL, 128), lambda *_: (0, NST // TAIL, 0))


PLACES = (pltpu.HBM, pltpu.VMEM)


def held(x):
    return pltpu.with_memory_space_constraint(x, pltpu.VMEM)


def far(x):
    return pltpu.with_memory_space_constraint(x, pltpu.HBM)


def call(body, outs, ins, out_specs, scratch=(), limit=16, flops=0, grid=(), alias=None):
    return pl.pallas_call(
        body,
        out_shape=[
            (PLACES[o[2]] if len(o) == 3 else jax.ShapeDtypeStruct)(o[0], o[1])
            for o in outs
        ],
        grid_spec=pl.GridSpec(
            grid=grid, in_specs=ins, out_specs=out_specs, scratch_shapes=list(scratch)
        ),
        compiler_params=pltpu.CompilerParams(vmem_limit_bytes=limit << 20),
        input_output_aliases=alias or {},
        cost_estimate=pl.CostEstimate(flops=flops, transcendentals=0, bytes_accessed=4 << 20),
    )


def local_end_body(
    core, x_far, wr_far, step_far, logd_far, pay, run_out, step_out, x, wr, step, logd, sem
):
    moves = [
        pltpu.make_async_copy(a, b, sem.at[k])
        for k, (a, b) in enumerate(
            ((logd_far, logd), (step_far, step), (wr_far, wr), (x_far, x))
        )
    ]
    del core
    for m in moves:
        m.start()
    moves[0].wait()
    moves[1].wait()
    ld = jnp.concatenate([logd[...], logd[...]], axis=0).T
    st = jnp.concatenate([step[...], step[...]], axis=0).T
    row = iota((TOK, 2 * HEADS), 0)
    run = ld
    s = 1
    while s < TOK:
        run = run + jnp.where(row >= s, pltpu.roll(run, s, 0), 0.0)
        s *= 2
    run_out[...] = run
    step_out[...] = st
    total = run[TOK - 1 : TOK, :]
    pair = split_pair(st * jnp.exp(total - run))
    t1 = total.astype(BF16).astype(F32)
    t2 = (total - t1).astype(BF16).astype(F32)
    t3 = total - t1 - t2
    trow = iota((TAIL, 2 * HEADS), 0)
    tails = jnp.where(trow == 0, t1, jnp.where(trow == 1, t2, jnp.where(trow == 2, t3, 0.0)))
    tails = jnp.where(iota((TAIL, 2 * HEADS), 1) < HEADS, tails, 0.0).astype(BF16)
    moves[2].wait()
    wt = turned(wr[...])
    base = spreader()
    moves[3].wait()
    for c in range(NCH):
        e = spread_of(base, c)
        xs = (x[:, cols(c)].astype(F32) * dot(pair, e)).astype(BF16)
        end = dot(wt, xs).astype(BF16)
        extra = dot(tails, e).astype(BF16)
        for k in range(2):
            lanes = slice(k * 128, (k + 1) * 128)
            pay[2 * c + k, 0:NST, :] = end[:, lanes]
            pay[2 * c + k, NST : NST + TAIL, :] = extra[:, lanes]


def decayed(tail):
    return jnp.exp(
        tail[0:1, :].astype(F32) + tail[1:2, :].astype(F32) + tail[2:3, :].astype(F32)
    )


def prefix_body(got, asks, local, pay):
    del local
    state = jnp.zeros((NST, 128), F32)
    for d in range(OWN):
        pay[d, 0:NST, :] = state.astype(BF16)
        pay[d, NST : NST + TAIL, :] = asks[d]
        if d < OWN - 1:
            decay = decayed(got[d, NST : NST + TAIL, :])
            state = decay * state + got[d, 0:NST, :].astype(F32)


def head_weights(run_rows, run_lanes, h, lanes, mask, aff, forward):
    a = run_rows[:, h : h + 1]
    b = run_lanes[h : h + 1, lanes]
    gap = a - b if forward else b - a
    return (jnp.exp2(jnp.where(mask, gap, NEG)) * aff).astype(BF16)


def lane_masks():
    which = iota((BLK, 128), 1) >> 5
    return [(which == q).astype(F32).astype(BF16) for q in range(4)]


def group_out(run_rows, run_lanes, first, lanes, mask, aff, values, masks, forward):
    ws = [
        head_weights(run_rows, run_lanes, first + q, lanes, mask, aff, forward) for q in range(4)
    ]
    return dot(
        jnp.concatenate(ws, axis=1), jnp.concatenate([values * m for m in masks], axis=0)
    )


def fore_local_body(x, wr, rd, run, step, out, mid):
    run2 = run[...] * LOG2E
    run_lanes = run2.T
    masks = lane_masks()
    mask = iota((BLK, BLK), 0) >= iota((BLK, BLK), 1)
    base = spreader()
    step_pair = split_pair(step[...])
    edge = run2[BLK - 1 : BLK, :]
    for b in range(2):
        rows = slice(b * BLK, (b + 1) * BLK)
        run_rows = run2[rows, :]
        aff = dot_t(rd[rows, :], wr[rows, :])
        if b == 0:
            side = split_pair(step[rows, :] * jnp.exp2(edge - run_rows))
            wt = turned(wr[rows, :])
        else:
            side = split_pair(jnp.exp2(run_rows - edge))
        for c in range(NCH):
            e = spread_of(base, c)
            xs = x[rows, cols(c)].astype(F32)
            values = (xs * dot(step_pair[rows, :], e)).astype(BF16)
            sides = dot(side, e)
            if b == 0:
                mid[:, cols(c)] = dot(wt, (xs * sides).astype(BF16)).astype(BF16)
            else:
                carried = sides * dot(rd[rows, :], mid[:, cols(c)])
            for k in range(2):
                lanes = slice(k * 128, (k + 1) * 128)
                o = group_out(
                    run_rows, run_lanes, 8 * c + 4 * k, rows, mask, aff, values[:, lanes], masks, True
                )
                if b == 1:
                    o = o + carried[:, lanes]
                out[rows, c * CH + k * 128 : c * CH + (k + 1) * 128] = o


def back_local_body(og, wr, rd, run, out, mid):
    run2 = run[...] * LOG2E
    run_lanes = run2.T
    masks = lane_masks()
    mask = iota((BLK, BLK), 0) <= iota((BLK, BLK), 1)
    base = spreader()
    edge = run2[BLK - 1 : BLK, :]
    for b in (1, 0):
        rows = slice(b * BLK, (b + 1) * BLK)
        run_rows = run2[rows, :]
        aff = dot_t(wr[rows, :], rd[rows, :])
        if b == 1:
            side = split_pair(jnp.exp2(run_rows - edge))
            rt = turned(rd[rows, :])
        else:
            side = split_pair(jnp.exp2(edge - run_rows))
        for c in range(NCH):
            e = spread_of(base, c)
            values = og[rows, cols(c)]
            sides = dot(side, e)
            if b == 1:
                mid[:, cols(c)] = dot(rt, (values.astype(F32) * sides).astype(BF16)).astype(BF16)
            else:
                carried = sides * dot(wr[rows, :], mid[:, cols(c)])
            for k in range(2):
                lanes = slice(k * 128, (k + 1) * 128)
                o = group_out(
                    run_rows, run_lanes, 8 * c + 4 * k, rows, mask, aff, values[:, lanes], masks, False
                )
                if b == 0:
                    o = o + carried[:, lanes]
                out[rows, c * CH + k * 128 : c * CH + (k + 1) * 128] = o


def back_local_when(which, core, og, wr, rd, run, *refs):
    far_out, out, mid, sem = refs[-4:]

    @pl.when(core[0] == which)
    def _():
        back_local_body(og, wr, rd, run, out, mid)
        move = pltpu.make_async_copy(out, far_out, sem.at[0])
        move.start()
        move.wait()


def back_local_early(*refs):
    back_local_when(0, *refs)


def back_local_late(*refs):
    back_local_when(1, *refs)


def places_body(ids, depth, count, camera, gain, asks, place_col, place_row, live, tile_gain):
    idv = ids[...].astype(F32)
    dep = depth[...]
    seq = jnp.zeros((SLOTS, TILES), F32)
    for s in range(SLOTS):
        seq = seq + jnp.where(dep == s, idv[s : s + 1, :], 0.0)
    seq = seq.T
    live[...] = jnp.where(dep < count[...], 0.95, 0.0).T
    hot = (iota((8, TILES), 0) == camera[...]).astype(F32).T
    vg = gain[...].T
    wide = iota((8, FEAT), 1)
    gains = jnp.where(wide < 64, vg[:, 0:1], jnp.where(wide < 128, vg[:, 1:2], vg[:, 2:3]))
    per_tile = jnp.zeros((TILES, FEAT), F32)
    for v in range(8):
        per_tile = per_tile + hot[:, v : v + 1] * gains[v : v + 1, :]
    tile_gain[...] = per_tile
    lane = iota((128, 128), 1)
    lane_f = lane.astype(F32)
    below = (iota((128, 128), 0) > lane).astype(F32).astype(BF16)
    seen = jnp.zeros((1, 128), F32)
    total = jnp.zeros((128, 128), F32)
    for b in range(ROWS // 128):
        two = [jnp.broadcast_to(seq[:, k : k + 1], (TILES, 128)) for k in (2 * b, 2 * b + 1)]
        token = jnp.concatenate(two, axis=0).astype(jnp.int32)
        owner = token >> 8
        local = (token & 255).astype(F32)
        hot = owner == lane
        hot_f = hot.astype(F32)
        rank = dot(below, hot_f.astype(BF16)) + seen
        seen = seen + jnp.sum(hot_f, axis=0, keepdims=True)
        mine = jnp.sum(jnp.where(hot, rank, 0.0), axis=1, keepdims=True)
        mine = jnp.broadcast_to(mine, (128, 128))
        place = mine + (owner * 128).astype(F32)
        place_col[b * 128 : (b + 1) * 128, :] = place
        place_row[:, b * 128 : (b + 1) * 128] = place.T[0:8, :]
        named = jnp.where(hot, local, 0.0)
        total = total + dot(turned(named), (mine == lane_f).astype(F32).astype(BF16))
    first = iota((TAIL, 128), 0) == 0
    for o in range(OWN):
        asks[o] = jnp.where(first, total[o : o + 1, :], 0.0).astype(BF16)


def features_body(local, got, rd, run, weight, scan_out, answer):
    base = spreader()
    lead = split_pair(jnp.exp(run[...]))
    asked = jnp.concatenate(
        [got[d, NST : NST + TAIL, :].astype(F32)[0:1, :] for d in range(OWN)]
        + [jnp.zeros((128 - OWN, 128), F32)],
        axis=0,
    ).T
    feat = jnp.zeros((TOK, FEAT), F32)
    for c in range(NCH):
        state = jnp.concatenate([got[2 * c, 0:NST, :], got[2 * c + 1, 0:NST, :]], axis=1)
        rows = local[:, cols(c)] + dot(lead, spread_of(base, c)) * dot(rd[...], state)
        rows = rows.astype(BF16)
        scan_out[:, cols(c)] = rows
        feat = feat + dot(rows, weight[cols(c), :])
    feat = feat.astype(BF16)
    token = iota((128, TOK), 1).astype(F32)
    for d in range(OWN):
        pick = (asked[:, d : d + 1] == token).astype(F32).astype(BF16)
        answer[d] = dot(pick, feat).astype(BF16)


def composite_body(
    ans, place_col, place_row, live, tile_gain, target, out, slots, keep, trans, grads
):
    one, zero = jnp.ones((256, 128), BF16), jnp.zeros((256, 128), BF16)
    lane_o = iota((256, 128), 1).astype(jnp.int16)
    for b in range(ROWS // 256):
        rows = slice(b * 256, (b + 1) * 256)
        place = place_col[rows, :].astype(jnp.int32).astype(jnp.int16)
        hot = jnp.concatenate(
            [jnp.where(place == lane_o + np.int16(128 * o), one, zero) for o in range(OWN)], axis=1
        )
        slots[rows, :] = dot(hot, ans[...])
    lane = iota((TILES, 128), 1)
    left = lane < GAUSS_LANES
    gain_a, gain_b = tile_gain[:, 0:128], tile_gain[:, 128:256]
    target_a = target[:, 0:128]
    target_b = jnp.concatenate([target[:, 128:192], jnp.zeros((TILES, 64), F32)], axis=1)
    t = jnp.ones((TILES, 128), F32)
    ra = jnp.zeros((TILES, 128), F32)
    rb = jnp.zeros((TILES, 128), F32)
    for k in range(SLOTS):
        rows = slice(k * TILES, (k + 1) * TILES)
        sa = jax.nn.sigmoid(slots[rows, 0:128])
        sb = jax.nn.sigmoid(slots[rows, 128:256])
        so = jnp.where(left, pltpu.roll(sb, 64, 1), sb)
        a = so * live[:, k : k + 1]
        w = t * a
        ra = ra + w * sa
        rb = rb + w * sb
        slots[rows, 0:128] = sa
        slots[rows, 128:256] = sb
        keep[rows, :] = so
        trans[rows, :] = t
        t = t * (1.0 - a)
    ea = ra * gain_a - target_a
    eb = rb * gain_b - target_b
    ga = ea * lax.rsqrt(ea * ea + 0.01) * gain_a
    gb = jnp.where(left, eb * lax.rsqrt(eb * eb + 0.01) * gain_b, 0.0)
    dt = jnp.zeros((TILES, 128), F32)
    for k in reversed(range(SLOTS)):
        rows = slice(k * TILES, (k + 1) * TILES)
        sa = slots[rows, 0:128]
        sb = slots[rows, 128:256]
        so = keep[rows, :]
        t = trans[rows, :]
        a = so * live[:, k : k + 1]
        ua = ga * sa
        ub = gb * sb
        q = ua + ub
        q = q + pltpu.roll(q, 64, 1)
        da = t * (q - dt)
        dt = a * q + (1.0 - a) * dt
        w = t * a
        grads[rows, 0:128] = (w * ua * (1.0 - sa)).astype(BF16)
        grads[rows, 128:256] = jnp.where(
            left, w * ub * (1.0 - sb), da * a * (1.0 - so)
        ).astype(BF16)
    sub_f = iota((256, ROWS), 0).astype(F32)
    place = place_row[0:1, :]
    for b in range(OWN * 128 // 256):
        hot = (place == sub_f + 256.0 * b).astype(F32).astype(BF16)
        out[b * 256 : (b + 1) * 256, :] = dot(hot, grads[...]).astype(BF16)


GAUSS_LANES = 64
HALF = 128


def token_grad_body(core, homed, asked, scan_out, low_out, mine, theirs):
    token = iota((TOK, 128), 0).astype(F32)
    hot = jnp.concatenate(
        [
            (asked[d].astype(F32)[0:1, :] == token).astype(F32).astype(BF16)
            for d in range(OWN)
        ],
        axis=1,
    )
    low = dot(hot, homed[...]).astype(BF16)
    low_out[...] = low
    low_t = turned(low)
    first = core[0] == 0
    upper, lower = low_t[0:HALF, :].astype(F32), low_t[HALF:FEAT, :].astype(F32)
    own = jnp.where(first, upper, lower).astype(BF16)
    far = jnp.where(first, lower, upper).astype(BF16)
    for c in range(NCH):
        for rows, out in ((far, theirs), (own, mine)):
            piece = dot(rows, scan_out[:, cols(c)]).astype(BF16)
            for k in range(2):
                out[2 * c + k] = piece[:, k * 128 : (k + 1) * 128]


def out_grad_body(low, weight, rd, run, out_grad, ends):
    base = spreader()
    lead = split_pair(jnp.exp(run[...]))
    rt = turned(rd[...])
    for c in range(NCH):
        og = dot_t(low[...], weight[cols(c), :]).astype(BF16)
        out_grad[:, cols(c)] = og
        scaled = (og.astype(F32) * dot(lead, spread_of(base, c))).astype(BF16)
        end = dot(rt, scaled).astype(BF16)
        for k in range(2):
            ends[2 * c + k] = end[:, k * 128 : (k + 1) * 128]


def join_body(ends, mine, other, within, pay):
    del within
    for g in range(OWN):
        pay[g, 0:NST, :] = ends[g]
        pay[g, NST : NST + HALF, :] = (mine[g].astype(F32) + other[g].astype(F32)).astype(BF16)


def scene_sum_body(got, part):
    total = jnp.zeros((HALF, 128), F32)
    for d in range(OWN):
        total = total + got[d, NST : NST + HALF, :].astype(F32)
    part[...] = total


def suffix_body(scale, got, tails, part, within, pay):
    del within
    state = jnp.zeros((NST, 128), F32)
    block = (part[...] * scale).T.astype(BF16)
    for d in reversed(range(OWN)):
        pay[d, 0:NST, :] = state.astype(BF16)
        pay[d, NST : NST + HALF, :] = block
        if d > 0:
            state = decayed(tails[d]) * state + got[d].astype(F32)


def join_weight_body(core, own, other, out):
    first = core[0] == 0
    for d in range(OWN):
        rows = slice(d * 128, (d + 1) * 128)
        a, b = own[d, NST : NST + HALF, :].astype(F32), other[d].astype(F32)
        out[rows, 0:HALF] = jnp.where(first, a, b)
        out[rows, HALF:FEAT] = jnp.where(first, b, a)


def input_grad_body(within, got, wr, run, step, grad):
    base = spreader()
    run_v = run[...]
    tail = split_pair(jnp.exp(run_v[TOK - 1 : TOK, :] - run_v))
    steps = split_pair(step[...])
    for c in range(NCH):
        e = spread_of(base, c)
        state = jnp.concatenate([got[2 * c, 0:NST, :], got[2 * c + 1, 0:NST, :]], axis=1)
        rows = within[:, cols(c)] + dot(tail, e) * dot(wr[...], state)
        grad[:, cols(c)] = (rows * dot(steps, e)).astype(BF16)


def swap(x, axes):
    return lax.all_to_all(x, axes, split_axis=0, concat_axis=0, tiled=True)


def shards(
    ssm_input,
    write_basis,
    read_basis,
    step_size,
    log_decay,
    head_weight,
    block_list,
    block_count,
    depth_order,
    camera_index,
    view_gain,
    target_color,
):
    x, wr, rd = ssm_input[0], write_basis[0], read_basis[0]
    buf = pltpu.VMEM
    scenes = lax.axis_size("dp")
    core = lax.axis_index("dp") % 2
    core_ref = core.astype(jnp.int32).reshape(1)

    def trade(v, hop):
        return lax.ppermute(v, "dp", [(i, i ^ hop) for i in range(scenes)])

    pay, run, step = call(
        local_end_body,
        [((OWN, NST + TAIL, 128), BF16), ((TOK, 128), F32, 1), ((TOK, 128), F32, 1)],
        [SMEM] + [ANY] * 4,
        [VMEM] * 3,
        scratch=[
            buf((TOK, WID), BF16),
            buf((TOK, NST), BF16),
            buf((HEADS, TOK), F32),
            buf((HEADS, TOK), F32),
            pltpu.SemaphoreType.DMA((4,)),
        ],
        flops=1 << 29,
    )(core_ref, far(x), far(wr), far(step_size[0].T), far(log_decay[0].T))
    ends = swap(pay, SEQ)
    asks, place_col, place_row, live, tile_gain = call(
        places_body,
        [
            ((OWN, TAIL, 128), BF16, 1),
            ((ROWS, 128), F32, 0),
            ((8, ROWS), F32, 0),
            ((TILES, SLOTS), F32, 0),
            ((TILES, FEAT), F32, 0),
        ],
        [VMEM] * 5,
        [VMEM] * 5,
        flops=1 << 31,
    )(block_list[0].T, depth_order[0].T, block_count, camera_index, view_gain[0].T)
    (local,) = call(
        fore_local_body,
        [((TOK, WID), F32, 0)],
        [VMEM] * 5,
        [VMEM],
        scratch=[buf((NST, WID), BF16)],
        flops=1 << 32,
    )(x, wr, rd, held(run), held(step))
    (pay,) = call(
        prefix_body, [((OWN, NST + TAIL, 128), BF16)], [VMEM, VMEM, ANY], [VMEM]
    )(ends, held(asks), far(local))
    states = swap(pay, SEQ)
    scan_out, answer = call(
        features_body,
        [((TOK, WID), BF16, 1), ((OWN, 128, FEAT), BF16)],
        [VMEM] * 5,
        [VMEM] * 2,
        flops=1 << 31,
    )(local, states, rd, held(run), head_weight)
    answered = swap(answer, SEQ)
    (outgoing,) = call(
        composite_body,
        [((OWN * 128, FEAT), BF16)],
        [VMEM] * 6,
        [VMEM],
        scratch=[
            buf((ROWS, FEAT), F32),
            buf((ROWS, 128), F32),
            buf((ROWS, 128), F32),
            buf((ROWS, FEAT), BF16),
        ],
        flops=1 << 32,
    )(
        answered.reshape(OWN * 128, FEAT),
        place_col,
        place_row,
        live,
        tile_gain,
        target_color[0],
    )
    homed = swap(outgoing.reshape(OWN, 128, FEAT), SEQ)
    low, mine, theirs = call(
        token_grad_body,
        [((TOK, FEAT), BF16, 1), ((OWN, HALF, 128), BF16), ((OWN, HALF, 128), BF16)],
        [SMEM, VMEM, TAIL_SPEC, VMEM],
        [VMEM] * 3,
        grid=(1,),
        flops=1 << 31,
    )(core_ref, homed.reshape(OWN * 128, FEAT), states, held(scan_out))
    other = trade(theirs, 1)
    out_grad, back_ends = call(
        out_grad_body,
        [((TOK, WID), BF16, 1), ((OWN, NST, 128), BF16, 1)],
        [VMEM] * 4,
        [VMEM, VMEM],
        flops=1 << 31,
    )(held(low), head_weight, rd, held(run))
    within_scratch = [
        buf((TOK, WID), F32),
        buf((NST, WID), BF16),
        pltpu.SemaphoreType.DMA((1,)),
    ]
    (within,) = call(
        back_local_early,
        [((TOK, WID), F32, 1)],
        [SMEM] + [VMEM] * 4,
        [ANY],
        scratch=within_scratch,
        flops=1 << 32,
    )(core_ref, held(out_grad), wr, rd, held(run))
    (pay,) = call(
        join_body, [((OWN, NST + HALF, 128), BF16)], [VMEM] * 3 + [ANY], [VMEM]
    )(held(back_ends), mine, other, held(within))
    back = swap(pay, SEQ)
    (within,) = call(
        back_local_late,
        [((TOK, WID), F32, 1)],
        [SMEM] + [VMEM] * 4 + [ANY],
        [ANY],
        scratch=within_scratch,
        flops=1 << 32,
        alias={5: 0},
    )(core_ref, held(out_grad), wr, rd, held(run), held(within))
    (part,) = call(scene_sum_body, [((HALF, 128), F32)], [VMEM], [VMEM])(back)
    part = (part + trade(part, 2)) + (trade(part, 4) + trade(part, 6))
    scale = np.float32(1.0 / np.sqrt(float(scenes * TOK * lax.axis_size(SEQ))))
    (pay,) = call(
        lambda *refs: suffix_body(scale, *refs),
        [((OWN, NST + HALF, 128), BF16)],
        [pl.BlockSpec((OWN, NST, 128), lambda *_: (0, 0, 0)), TAIL_SPEC, VMEM, ANY],
        [VMEM],
        grid=(1,),
    )(back, ends, part, within)
    last = swap(pay, SEQ)
    other = trade(last[:, NST:, :], 1)
    (grad,) = call(
        input_grad_body, [((TOK, WID), BF16)], [VMEM] * 5, [VMEM], flops=1 << 30
    )(held(within), last, wr, held(run), held(step))
    (wgrad,) = call(
        join_weight_body, [((WID, FEAT), F32)], [SMEM, VMEM, VMEM], [VMEM]
    )(core_ref, last, other)
    return grad[None], wgrad


def solution(mesh):
    torus = Mesh(mesh.devices.reshape(mesh.shape["dp"], 4, 4), ("dp", "seq_0", "seq_1"))
    in_specs = (
        P("dp", SEQ, None),
        P("dp", SEQ, None),
        P("dp", SEQ, None),
        P("dp", SEQ, None),
        P("dp", SEQ, None),
        P(),
        P("dp", SEQ, None),
        P("dp", SEQ),
        P("dp", SEQ, None),
        P("dp", SEQ),
        P("dp", None, None),
        P("dp", SEQ, None),
    )
    out_specs = (P("dp", SEQ, None), P())
    return jax.shard_map(
        shards, mesh=torus, in_specs=in_specs, out_specs=out_specs, check_vma=False
    )
```
